512 devices in a mesh: gx: 32 (over x, z), gy: 4 (over y_lo), chaos: 4 (over y_hi, core).
Axes of the slice: x: 4, y: 8 (y_hi: 2, y_lo: 4; y = y_hi * 4 + y_lo), z: 8, core: 2. Of those that a mesh axis runs over, the one named last changes fastest.
Arguments:
- field: float32 [68, 128, 32, 128], P('chaos', 'gx', 'gy'), may hold values from -6 to 6
- source: float32 [68, 128, 32, 128], P('chaos', 'gx', 'gy'), may hold values from -6 to 6
- mean_coef: float32 [128, 32, 128], P('gx', 'gy'), may hold values from 1 to 3
- var_coefs: float32 [10, 128, 32, 128], P(None, 'gx', 'gy'), may hold values from -0.6 to 0.6
- galerkin_cols: int32 [10, 68, 3], replicated, may hold values from 0 to 65
- galerkin_vals: float32 [10, 68, 3], replicated, may hold values from -3 to 3
Outputs:
- smoothed: float32 [68, 128, 32, 128], P('chaos', 'gx', 'gy')
- coarse_residual: float32 [68, 64, 16, 64], P('chaos', 'gx', 'gy')
The draws below stay inside these ranges and needn't reach their ends.
All inputs are finite; a program needn't handle non-finite values.
Results may differ from the reference program's by a relative error of at most 0.0001.
Values sent between devices are 32-bit elements; how exact they have to be, the bound alone decides.
A program may use at most 128 MiB of HBM per device.

```python
import math
import jax
import jax.numpy as jnp
from jax import lax

P_SIZE = 66
VARS = 10
NB = 3
SLOTS = 68
NX = 128
NY = 32
NZ = 128


def touch_ends(values, stream_key, smallest, largest):
    place = [jax.random.randint(jax.random.fold_in(stream_key, axis), (), 0, length) for axis, length in enumerate(values.shape)]
    widest = values.shape.index(max(values.shape))
    beside = place[:widest] + [(place[widest] + 1) % values.shape[widest]] + place[widest + 1:]
    return values.at[tuple(place)].set(smallest).at[tuple(beside)].set(largest)


def block_levels(rng, shape, split, smallest, high):
    def one(dim, blocks):
        steps = jax.random.uniform(jax.random.fold_in(jax.random.fold_in(rng, 6), dim), (blocks,), jnp.float32, smallest / len(split), high / len(split))
        return jnp.repeat(jnp.exp(steps), shape[dim] // blocks).reshape((-1,) + (1,) * (len(shape) - dim - 1))

    factor_of = one(*split[0])
    for cut in split[1:]:
        factor_of = factor_of * one(*cut)
    return factor_of


def gaussian(rng, extent, deviation, bound, shards=(), kind=jnp.bfloat16):
    loudness = block_levels(rng, extent, shards, -0.22, 0.18) if shards else 1.0
    values = jax.random.normal(rng, extent, jnp.float32) * deviation * loudness
    return jnp.minimum(jnp.maximum(values, -bound), bound).astype(kind)


def setup_inputs(seed: int = 0) -> dict:
    arg_keys = jax.random.split(jax.random.key(seed), 7)
    field = gaussian(arg_keys[0], (SLOTS, NX, NY, NZ), 1.0, 6.0, ((0, 4), (1, 32), (2, 4)), jnp.float32)
    source = gaussian(arg_keys[1], (SLOTS, NX, NY, NZ), 1.0, 6.0, ((0, 4), (1, 32), (2, 4)), jnp.float32)
    mean_coef = jnp.clip(jnp.exp(math.log(3.0) - 1.0986123 * jax.random.uniform(arg_keys[2], (NX, NY, NZ), jnp.float32) ** block_levels(arg_keys[2], (NX, NY, NZ), ((0, 32), (1, 4)), -0.2, 0.2)), 1.0, 3.0)
    var_coefs = jnp.clip(jax.random.uniform(arg_keys[3], (VARS, NX, NY, NZ), jnp.float32, -0.6, 0.6) * block_levels(arg_keys[3], (VARS, NX, NY, NZ), ((1, 32), (2, 4)), -0.4, 0.0), -0.6, 0.6)
    galerkin_cols = touch_ends(jax.random.randint(arg_keys[4], (VARS, SLOTS, NB), 0, P_SIZE), jax.random.fold_in(arg_keys[4], 1), 0, P_SIZE - 1).astype(jnp.int32)
    galerkin_vals = gaussian(arg_keys[5], (VARS, SLOTS, NB), 0.5, 3.0, (), jnp.float32)
    return {"field": field, "source": source, "mean_coef": mean_coef, "var_coefs": var_coefs, "galerkin_cols": galerkin_cols, "galerkin_vals": galerkin_vals}


def build_mixing(galerkin_cols, galerkin_vals):
    slots = galerkin_cols.shape[1]
    match = (galerkin_cols[..., None] == jnp.arange(slots, dtype=jnp.int32)).astype(jnp.float32)
    return jnp.sum(match * galerkin_vals[..., None], axis=2)


def laplace(field):
    padded = jnp.pad(field, ((0, 0), (1, 1), (1, 1), (1, 1)))
    beside = padded[:, 2:, 1:-1, 1:-1] + padded[:, :-2, 1:-1, 1:-1]
    beside = beside + padded[:, 1:-1, 2:, 1:-1] + padded[:, 1:-1, :-2, 1:-1]
    beside = beside + padded[:, 1:-1, 1:-1, 2:] + padded[:, 1:-1, 1:-1, :-2]
    return 6.0 * field - beside


def operate(field, mean_coef, var_coefs, mixing):
    lap = laplace(field)
    flat = lap.reshape(lap.shape[0], -1)

    def step(total, inputs):
        matrix, coef = inputs
        mixed = jnp.dot(matrix, flat, precision=lax.Precision.HIGHEST).reshape(lap.shape)
        return total + coef[None] * mixed, None

    coupled, unused = lax.scan(step, jnp.zeros(lap.shape, jnp.float32), (mixing, var_coefs))
    return mean_coef[None] * lap + coupled


def halve(values, axis):
    even = lax.slice_in_dim(values, 0, values.shape[axis], 2, axis)
    odd = lax.slice_in_dim(values, 1, values.shape[axis], 2, axis)
    lower = lax.slice_in_dim(odd, 0, odd.shape[axis] - 1, 1, axis)
    prev = jnp.concatenate([jnp.zeros_like(lax.slice_in_dim(odd, 0, 1, 1, axis)), lower], axis)
    return 0.5 * even + 0.25 * (odd + prev)


def reference(field, source, mean_coef, var_coefs, galerkin_cols, galerkin_vals):
    slots = field.shape[0]
    mask = (jnp.arange(slots, dtype=jnp.int32) < P_SIZE).astype(jnp.float32)[:, None, None, None]
    mixing = build_mixing(galerkin_cols, galerkin_vals)
    start = mask * field
    first = source - operate(start, mean_coef, var_coefs, mixing)
    smoothed = mask * (start + (2.0 / 3.0) * first / (6.0 * mean_coef[None]))
    after = mask * (source - operate(smoothed, mean_coef, var_coefs, mixing))
    coarse = halve(halve(halve(after, 1), 2), 3)
    return smoothed, coarse
```

```python
import jax
import jax.numpy as jnp
from jax import lax
from jax.experimental import pallas as pl
from jax.experimental.pallas import tpu as pltpu
from jax.sharding import PartitionSpec as P


P_SIZE = 66
MESH = pl.DeviceIdType.MESH
SL = 17
OWN = 136
VEC = 72
ALL = 8 * VEC
TERMS = 10
KSEG = 80
F32 = jnp.float32
BF16 = jnp.bfloat16


def lanes(rows):
    return lax.broadcasted_iota(jnp.int32, (rows, 128), 1)


def swing(a):
    return pltpu.roll(a, 64, 1)


def kernel(
    field, source, mean, var, cols, vals, smoothed, coarse,
    fs, ss, cs, fr, sr, cr, v1, v2, xlo1, xhi1, ylo1, yhi1, z1, xlo2, xhi2, ylo2, yhi2, z2,
    ysend1, ysend2, lap, rhs, left, left16, gt, gt2, srcv, after, wz, bs, br, dbuf, cxs, cys, cxr, cyr, cxyr, fin, cbs, cbr,
    send, recv,
):
    gx, gy, ch = lax.axis_index("gx"), lax.axis_index("gy"), lax.axis_index("chaos")
    hi, core = ch // 2, ch % 2
    chip = hi * 4 + gy
    pos = (chip + 6) % 8
    side, blk = pos // 4, pos % 4
    xi = gx * 2 + core
    last_x = 2 * lax.axis_size("gx") - 1

    far_gy = (gy + 2) % 4

    def worker(s, c):
        return (gx, far_gy, (((gy + 2 + 4 * s) % 8) // 4) * 2 + c)

    def owner(j):
        return (gx, far_gy, j)

    def place(dx, dy):
        x, d = xi + dx, (chip + dy + 8) % 8
        return (x // 2, d % 4, (d // 4) * 2 + x % 2)

    has_xp, has_xn = xi > 0, xi < last_x
    has_yp, has_yn = blk > 0, blk < 3
    across = (gx, gy, (1 - hi) * 2 + core)

    barrier = pltpu.get_barrier_semaphore()
    neighbours = [
        (has_xp, place(-1, 0)), (has_xn, place(1, 0)), (has_yp, place(0, -1)), (has_yn, place(0, 1)),
        (jnp.logical_and(has_xp, has_yp), place(-1, -1)), (jnp.logical_and(has_xn, has_yn), place(1, 1)),
    ]
    for j in range(4):
        pl.semaphore_signal(barrier, inc=1, device_id=owner(j), device_id_type=MESH)
    pl.semaphore_signal(barrier, inc=1, device_id=across, device_id_type=MESH)
    for cond, dev in neighbours:
        @pl.when(cond)
        def _():
            pl.semaphore_signal(barrier, inc=1, device_id=dev, device_id_type=MESH)

    keep = (lax.broadcasted_iota(jnp.int32, (16, 128), 0) + SL * ch < P_SIZE)
    keep_tail = SL * ch + 16 < P_SIZE
    low16, low8 = lanes(16) < 64, lanes(8) < 64

    def tails(t):
        r = pltpu.roll(swing(t), 4, 0)
        return jnp.where(low8, t, r), swing(jnp.where(low8, r, t))

    def pack(ref, out):
        for x in range(4):
            c, xl = x // 2, x % 2
            for y in range(4):
                v = xl * 4 + y
                a = jnp.where(keep, ref[pl.ds(x * 8 + y, 16, stride=32), :], 0.0)
                b = swing(jnp.where(keep, ref[pl.ds(x * 8 + y + 4, 16, stride=32), :], 0.0))
                out[pl.ds(c * OWN + v * 16, 16), :] = jnp.where(low16, a, b)
                out[pl.ds((2 + c) * OWN + v * 16, 16), :] = swing(jnp.where(low16, b, a))
            ta, tb = tails(jnp.where(keep_tail, ref[pl.ds(512 + x * 8, 8), :], 0.0))
            out[pl.ds(c * OWN + 128 + xl * 4, 4), :] = ta[0:4]
            out[pl.ds((2 + c) * OWN + 128 + xl * 4, 4), :] = tb[0:4]

    def piece(ref, i):
        return ref.at[pl.ds(pl.multiple_of(i * OWN, 8), OWN), :]

    def copy(src, dst, k, l, dev):
        return pltpu.make_async_remote_copy(
            src_ref=src, dst_ref=dst, send_sem=send.at[k], recv_sem=recv.at[l], device_id=dev, device_id_type=MESH
        )

    pack(field, fs)
    pl.semaphore_wait(barrier, 5 + sum(jnp.where(cond, 1, 0) for cond, dev in neighbours))

    for c in range(2):
        for s in range(2):
            copy(piece(fs, 2 * s + c), piece(fr, ch), 2 * s + c, ch, worker(s, c)).start()

    for k in range(TERMS + 1):
        for xl in range(2):
            if k < TERMS:
                t = var[pl.ds(pl.multiple_of(k * 32 + core * 16 + xl * 8, 8), 8), :]
            else:
                t = mean[pl.ds(pl.multiple_of(core * 16 + xl * 8, 8), 8), :]
            ta, tb = tails(t)
            cs[pl.ds(k * 8 + xl * 4, 4), :] = jnp.where(hi == 0, ta, tb)[0:4]
    coefs = copy(cs, cr, 8, 8, worker(hi, core))
    coefs.start()

    pack(source, ss)
    for c in range(2):
        for s in range(2):
            copy(piece(ss, 2 * s + c), piece(sr, ch), 4 + 2 * s + c, 4 + ch, worker(s, c)).start()

    zero_vec = jnp.zeros((VEC, 128), F32)
    for cond, xref, yref in ((xi == 0, (xlo1, xlo2), ()), (xi == last_x, (xhi1, xhi2), ()),
                             (blk == 0, (), (ylo1, ylo2)), (blk == 3, (), (yhi1, yhi2))):
        @pl.when(cond)
        def _():
            for ref in xref:
                for i in range(4):
                    ref[pl.ds(i * VEC, VEC), :] = zero_vec
            for ref in yref:
                ref[...] = zero_vec

    @pl.when(xi == 0)
    def _():
        cxr[...] = jnp.zeros((2 * VEC, 128), F32)

    @pl.when(blk == 0)
    def _():
        cyr[...] = zero_vec

    @pl.when(jnp.logical_or(xi == 0, blk == 0))
    def _():
        cxyr[...] = zero_vec

    rhs[...] = jnp.zeros((4 * 256, 256), BF16)
    gt[...] = jnp.zeros((128, 128), F32)
    p = lax.broadcasted_iota(jnp.int32, (KSEG, 68), 0)
    slot = jnp.where(p < 64, SL * lax.shift_right_logical(p, 4) + jnp.bitwise_and(p, 15),
                     jnp.where(p < 68, SL * (p - 64) + 16, -1))
    used = lax.broadcasted_iota(jnp.int32, (1, 68), 1) < P_SIZE
    lane72 = lanes(VEC)

    def build(k, carry):
        total = jnp.zeros((KSEG, 68), F32)
        for b in range(3):
            total = total + jnp.where(slot == cols[k, b:b + 1, :], jnp.where(used, vals[k, b:b + 1, :], 0.0), 0.0)
        gt[0:KSEG, 0:68] = total
        gt2[...] = jnp.transpose(gt[...])
        rows = [gt2[pl.ds(SL * j, 16), :] for j in range(4)]
        rows.append(gt2[pl.ds(16, 4, stride=SL), :])
        rows.append(jnp.zeros((4, 128), F32))
        g = jnp.concatenate(rows, 0)
        a1 = g.astype(BF16).astype(F32)
        a2 = g - a1
        r = pltpu.roll(a1, KSEG, 1)
        left[pl.ds(pl.multiple_of(k * VEC, 8), VEC), 0:128] = jnp.where(lane72 < 80, a1, r)
        left[pl.ds(pl.multiple_of(k * VEC, 8), VEC), 128:256] = jnp.where(lane72 < 32, r, pltpu.roll(a2, 32, 1))
        return carry

    lax.fori_loop(0, TERMS, build, 0)
    left16[...] = left[...].astype(BF16)

    row = lax.broadcasted_iota(jnp.int32, (256, 256), 0)
    col = lax.broadcasted_iota(jnp.int32, (256, 256), 1)
    half = jnp.bitwise_and(lax.shift_right_logical(row, 6), 1)
    b_row = 2 * half + lax.shift_right_logical(row, 7)
    z_row = jnp.bitwise_and(row, 63)
    off = z_row - 2 * jnp.bitwise_and(col, 31)
    near = jnp.where(off == 0, 0.5, jnp.where(jnp.logical_or(off == 1, off == -1), 0.25, 0.0))
    main_w = jnp.where(jnp.logical_and(col < 128, lax.shift_right_logical(col, 5) == b_row), near, 0.0)
    next_w = jnp.where(jnp.logical_and(col == 128 + b_row, z_row == 63), 0.25, 0.0)
    wz[...] = (main_w + next_w).astype(BF16)

    low = lane72 < 64
    z64 = jnp.bitwise_and(lane72, 63)
    edge = 63 * (1 - side)
    edge_lane = z64 == edge
    first_lane, end_lane = z64 == 0, z64 == 63

    def vec(ref, v):
        return ref[pl.ds(v * VEC, VEC), :]

    def gather(src, dst):
        for v in range(8):
            for j in range(4):
                dst[pl.ds(v * VEC + 16 * j, 16), :] = src[pl.ds(j * OWN + 16 * v, 16), :]
            dst[pl.ds(v * VEC + 64, 4), :] = src[pl.ds(128 + v, 4, stride=OWN), :]
            dst[pl.ds(v * VEC + 68, 4), :] = jnp.zeros((4, 128), F32)

    def arrived(dst, k, l):
        copy(dst, dst, k, l, across).wait_recv()

    def spread(val, stage, halos, base):
        xlo, xhi, ylo, yhi, z = halos
        up = stage.at[pl.ds(0, VEC), :]
        down = stage.at[pl.ds(VEC, VEC), :]
        zs = stage.at[pl.ds(2 * VEC, VEC), :]
        xn = copy(val.at[pl.ds(4 * VEC, 4 * VEC), :], xlo, base, base, place(1, 0))
        xp = copy(val.at[pl.ds(0, 4 * VEC), :], xhi, base + 1, base + 1, place(-1, 0))
        yn = copy(up, ylo, base + 2, base + 2, place(0, 1))
        yp = copy(down, yhi, base + 3, base + 3, place(0, -1))
        zc = copy(zs, z, base + 4, base + 4, across)

        total = zero_vec
        for v in range(8):
            total = jnp.where(z64 == v, pltpu.roll(vec(val, v), v + 65 * (1 - side), 1), total)
        zs[...] = total
        zc.start()

        @pl.when(has_xn)
        def _():
            xn.start()

        @pl.when(has_xp)
        def _():
            xp.start()

        up[...] = jnp.where(low, swing(vec(val, 3)), vec(val, 7))
        down[...] = jnp.where(low, vec(val, 0), swing(vec(val, 4)))

        @pl.when(has_yn)
        def _():
            yn.start()

        @pl.when(has_yp)
        def _():
            yp.start()

        return xn, xp, yn, yp, zc

    def collect(ops):
        xn, xp, yn, yp, zc = ops

        @pl.when(has_xp)
        def _():
            xn.wait_recv()

        @pl.when(has_xn)
        def _():
            xp.wait_recv()

        @pl.when(has_yp)
        def _():
            yn.wait_recv()

        @pl.when(has_yn)
        def _():
            yp.wait_recv()

        zc.wait_recv()

    def laplace(val, halos):
        xlo, xhi, ylo, yhi, z = halos
        for x in range(2):
            for y in range(4):
                v = 4 * x + y
                here = vec(val, v)
                beside = (vec(val, v - 4) if x else vec(xlo, y)) + (vec(xhi, y) if x else vec(val, v + 4))
                if y > 0:
                    beside = beside + vec(val, v - 1)
                elif x == 0:
                    beside = beside + jnp.where(low, ylo[...], swing(vec(val, 3)))
                else:
                    beside = beside + swing(jnp.where(low, vec(val, 7), ylo[...]))
                if y < 3:
                    beside = beside + vec(val, v + 1)
                elif x == 0:
                    beside = beside + swing(jnp.where(low, yhi[...], vec(val, 0)))
                else:
                    beside = beside + jnp.where(low, swing(vec(val, 4)), yhi[...])
                beside = beside + jnp.where(first_lane, 0.0, pltpu.roll(here, 1, 1))
                beside = beside + jnp.where(end_lane, 0.0, pltpu.roll(here, 127, 1))
                beside = beside + jnp.where(edge_lane, pltpu.roll(z[...], (edge + 128 - v) % 128, 1), 0.0)
                out = 6.0 * here - beside
                lap[pl.ds(v * VEC, VEC), :] = out
                b1 = out.astype(BF16)
                b2 = (out - b1.astype(F32)).astype(BF16)
                r, h = (v // 2) * 256, (v % 2) * 128
                rhs[r:r + VEC, h:h + 128] = b1
                rhs[r + KSEG:r + KSEG + VEC, h:h + 128] = b2
                rhs[r + 2 * KSEG:r + 2 * KSEG + VEC, h:h + 128] = b1

    def operate(use):
        def step(q, carry):
            mixed = jnp.dot(
                left16[...], rhs[pl.ds(pl.multiple_of(q * 256, 256), 256), :], preferred_element_type=F32
            )
            for h in range(2):
                v = 2 * q + h
                rows = pl.ds(pl.multiple_of(v * VEC, 8), VEC)
                m = cr[pl.ds(TERMS * 8 + v, 1), :]
                total = m * lap[rows, :]
                for k in range(TERMS):
                    total = total + cr[pl.ds(k * 8 + v, 1), :] * mixed[k * VEC:(k + 1) * VEC, h * 128:(h + 1) * 128]
                use(rows, m, total)
            return carry

        lax.fori_loop(0, 4, step, 0)

    for j in range(4):
        arrived(piece(fr, j), j, j)
    gather(fr, v1)
    halos1 = (xlo1, xhi1, ylo1, yhi1, z1)
    ops1 = spread(v1, ysend1, halos1, 9)
    arrived(cr, 8, 8)
    collect(ops1)
    laplace(v1, halos1)
    for j in range(4):
        arrived(piece(sr, j), 4 + j, 4 + j)
    gather(sr, srcv)

    def relax(rows, m, total):
        first = srcv[rows, :] - total
        v2[rows, :] = v1[rows, :] + (2.0 / 3.0) * first / (6.0 * m)

    operate(relax)

    halos2 = (xlo2, xhi2, ylo2, yhi2, z2)
    ops2 = spread(v2, ysend2, halos2, 14)
    for j in range(4):
        for v in range(8):
            bs[pl.ds(j * OWN + 16 * v, 16), :] = v2[pl.ds(v * VEC + 16 * j, 16), :]
        bs[pl.ds(j * OWN + 128, 8), :] = v2[pl.ds(64 + j, 8, stride=VEC), :]
    here = 2 * side + core
    for j in range(4):
        copy(piece(bs, j), piece(br, here), 19 + j, 19 + here, owner(j)).start()
    collect(ops2)
    laplace(v2, halos2)

    def residual(rows, m, total):
        after[rows, :] = srcv[rows, :] - total

    operate(residual)

    for i in range(2):
        if i == 0:
            c = [0.5 * vec(after, y) + 0.25 * vec(after, 4 + y) for y in range(4)]
        else:
            c = [0.25 * vec(after, 4 + y) for y in range(4)]
        s3 = 0.25 * swing(c[3])
        d0 = 0.5 * c[0] + 0.25 * c[1] + jnp.where(low, 0.0, s3)
        d1 = 0.5 * c[2] + 0.25 * (c[3] + c[1])
        dn = jnp.where(low, s3, 0.0)
        for r, (da, db) in ((i, (d0, d1)), (2 + i, (dn, None))):
            for h, d in ((0, da), (1, db)):
                if d is None:
                    d = zero_vec
                dh = d.astype(BF16)
                dbuf[pl.ds(r * VEC, VEC), h * 128:(h + 1) * 128] = dh.astype(F32)
                dbuf[pl.ds((4 + r) * VEC, VEC), h * 128:(h + 1) * 128] = d - dh.astype(F32)
    parts = jnp.dot(dbuf[...].astype(BF16), wz[...], preferred_element_type=F32)
    parts = parts[0:4 * VEC] + parts[4 * VEC:8 * VEC]

    def both(r):
        return parts[r * VEC:(r + 1) * VEC, 0:128], parts[r * VEC:(r + 1) * VEC, 128:256]

    def one(r):
        a, b = both(r)
        return a + pltpu.roll(b, 32, 1)

    a, b = both(1)
    cxs[0:VEC, :] = a
    cxs[VEC:2 * VEC, :] = b
    cx = copy(cxs, cxr, 23, 23, place(1, 0))

    @pl.when(has_xn)
    def _():
        cx.start()

    cys[0:VEC, :] = one(2)
    cys[VEC:2 * VEC, :] = one(3)
    cy = copy(cys.at[pl.ds(0, VEC), :], cyr, 24, 24, place(0, 1))
    cxy = copy(cys.at[pl.ds(VEC, VEC), :], cxyr, 25, 25, place(1, 1))

    @pl.when(has_yn)
    def _():
        cy.start()

    @pl.when(jnp.logical_and(has_xn, has_yn))
    def _():
        cxy.start()

    for j in range(4):
        arrived(piece(br, j), 19 + j, 19 + j)
    for x in range(4):
        c, xl = x // 2, x % 2
        for y in range(4):
            v = 4 * xl + y
            va = br[pl.ds(c * OWN + 16 * v, 16), :]
            vb = br[pl.ds((2 + c) * OWN + 16 * v, 16), :]
            smoothed[pl.ds(x * 8 + y, 16, stride=32), :] = jnp.where(low16, va, swing(vb))
            smoothed[pl.ds(x * 8 + y + 4, 16, stride=32), :] = jnp.where(low16, swing(va), vb)
        ta = br[pl.ds(c * OWN + 128, 8), :]
        tb = br[pl.ds((2 + c) * OWN + 128, 8), :]
        smoothed[pl.ds(512 + x * 8, 4), :] = jnp.where(low8, ta, swing(tb))[4 * xl:4 * xl + 4]
        smoothed[pl.ds(512 + x * 8 + 4, 4), :] = jnp.where(low8, swing(ta), tb)[4 * xl:4 * xl + 4]

    a, b = both(0)

    @pl.when(has_xp)
    def _():
        cx.wait_recv()

    @pl.when(has_yp)
    def _():
        cy.wait_recv()

    @pl.when(jnp.logical_and(has_xp, has_yp))
    def _():
        cxy.wait_recv()

    ysum = cyr[...] + cxyr[...]
    fin[0:VEC, :] = a + cxr[0:VEC, :] + jnp.where(lane72 < 32, ysum, 0.0)
    fin[VEC:2 * VEC, :] = b + cxr[VEC:2 * VEC, :] + jnp.where(lane72 == 0, pltpu.roll(ysum, 96, 1), 0.0)
    for j in range(4):
        cbs[pl.ds(j * 40, 16), :] = fin[pl.ds(16 * j, 16), :]
        cbs[pl.ds(j * 40 + 16, 16), :] = fin[pl.ds(VEC + 16 * j, 16), :]
        cbs[pl.ds(j * 40 + 32, 2), :] = fin[pl.ds(64 + j, 2, stride=VEC), :]
        cbs[pl.ds(j * 40 + 34, 6), :] = jnp.zeros((6, 128), F32)

    def small(ref, i):
        return ref.at[pl.ds(pl.multiple_of(i * 40, 8), 40), :]

    for j in range(4):
        copy(small(cbs, j), small(cbr, here), 26 + j, 26 + here, owner(j)).start()
    for j in range(4):
        arrived(small(cbr, j), 26 + j, 26 + j)
    lane16 = lanes(16)
    for x in range(2):
        ma, mb = cbr[pl.ds(x * 40, 16), :], cbr[pl.ds((2 + x) * 40, 16), :]
        za = cbr[pl.ds(x * 40 + 16, 16), :]
        tl, tr = cbr[pl.ds(x * 40 + 32, 8), :], cbr[pl.ds((2 + x) * 40 + 32, 8), :]
        for b in range(4):
            def joined(left_, right_, extra, lane):
                out = jnp.where(lane < 32, pltpu.roll(left_, (128 - 32 * b) % 128, 1), pltpu.roll(right_, (160 - 32 * b) % 128, 1))
                return out + jnp.where(lane == 32, pltpu.roll(extra, 32 - b, 1), 0.0)

            coarse[pl.ds(x * 4 + b, 16, stride=8), :] = joined(ma, mb, za, lane16)
            t = joined(tl, tr, pltpu.roll(tl, 7, 0), lanes(8))
            coarse[pl.ds(128 + x * 4 + b, 1), :] = t[0:1]

    for j in range(4):
        copy(piece(fs, j), piece(fr, j), j, j, across).wait_send()
        copy(piece(ss, j), piece(sr, j), 4 + j, 4 + j, across).wait_send()
        copy(piece(bs, j), piece(br, j), 19 + j, 19 + j, across).wait_send()
        copy(small(cbs, j), small(cbr, j), 26 + j, 26 + j, across).wait_send()
    coefs.wait_send()
    for xn, xp, yn, yp, zc in (ops1, ops2):
        zc.wait_send()
        for cond, op in ((has_xn, xn), (has_xp, xp), (has_yn, yn), (has_yp, yp)):
            @pl.when(cond)
            def _():
                op.wait_send()
    for cond, op in ((has_xn, cx), (has_yn, cy), (jnp.logical_and(has_xn, has_yn), cxy)):
        @pl.when(cond)
        def _():
            op.wait_send()


def scratch():
    def rows(n, width=128, kind=F32):
        return pltpu.VMEM((n, width), kind)

    halos = [rows(4 * VEC), rows(4 * VEC), rows(VEC), rows(VEC), rows(VEC)]
    return [
        rows(4 * OWN), rows(4 * OWN), rows(8 * (TERMS + 1)), rows(4 * OWN), rows(4 * OWN), rows(8 * (TERMS + 1)),
        rows(ALL), rows(ALL), *halos, *halos, rows(3 * VEC), rows(3 * VEC), rows(ALL), rows(4 * 256, 256, BF16),
        rows(TERMS * VEC, 256), rows(TERMS * VEC, 256, BF16), rows(128), rows(128), rows(ALL), rows(ALL), rows(256, 256, BF16),
        rows(4 * OWN), rows(4 * OWN), rows(8 * VEC, 256), rows(2 * VEC), rows(2 * VEC), rows(2 * VEC), rows(VEC),
        rows(VEC), rows(2 * VEC), rows(160), rows(160),
        pltpu.SemaphoreType.DMA((30,)), pltpu.SemaphoreType.DMA((30,)),
    ]


def body(field, source, mean_coef, var_coefs, galerkin_cols, galerkin_vals):
    whole = pl.BlockSpec(memory_space=pltpu.VMEM)
    smoothed, coarse = pl.pallas_call(
        kernel,
        out_shape=(jax.ShapeDtypeStruct((SL * 32, 128), F32), jax.ShapeDtypeStruct((SL * 8, 128), F32)),
        in_specs=[whole] * 6,
        out_specs=(whole, whole),
        scratch_shapes=scratch(),
        compiler_params=pltpu.CompilerParams(collective_id=0, has_side_effects=True),
        name="sweep",
    )(
        field.reshape(SL * 32, 128), source.reshape(SL * 32, 128), mean_coef.reshape(32, 128),
        var_coefs.reshape(TERMS * 32, 128), jnp.swapaxes(galerkin_cols, 1, 2), jnp.swapaxes(galerkin_vals, 1, 2),
    )
    return smoothed.reshape(field.shape), coarse[:, 0:64].reshape(SL, 2, 4, 64)


def solution(mesh):
    wide = P("chaos", "gx", "gy", None)
    return jax.shard_map(
        body,
        mesh=mesh,
        in_specs=(wide, wide, P("gx", "gy", None), P(None, "gx", "gy", None), P(), P()),
        out_specs=(wide, wide),
        check_vma=False,
    )
```

```python
import jax
import jax.numpy as jnp
from jax import lax
from jax.experimental import pallas as pl
from jax.experimental.pallas import tpu as pltpu
from jax.sharding import PartitionSpec as P


P_SIZE = 66
MESH = pl.DeviceIdType.MESH
SL = 17
OWN = 136
VEC = 72
ALL = 8 * VEC
TERMS = 10
KSEG = 80
F32 = jnp.float32
BF16 = jnp.bfloat16


def lanes(rows):
    return lax.broadcasted_iota(jnp.int32, (rows, 128), 1)


def swing(a):
    return pltpu.roll(a, 64, 1)


def kernel(
    field_in, source_in, mean_in, var_in, cols_in, vals_in, smoothed, coarse,
    field, source, mean, var, cols, vals, loads,
    fs, ss, cs, fr, sr, cr, v1, v2, xlo1, xhi1, ylo1, yhi1, z1, xlo2, xhi2, ylo2, yhi2, z2, zfull,
    ysend1, ysend2, lap, rhs, left, left16, gt, gt2, srcv, after, wz, bs, br, dbuf, cxs, cys, cxr, cyr, cxyr, fin, cbs, cbr,
    send, recv,
):
    gx, gy, ch = lax.axis_index("gx"), lax.axis_index("gy"), lax.axis_index("chaos")
    hi, core = ch // 2, ch % 2
    chip = hi * 4 + gy
    pos = (chip + 6) % 8
    side, blk = pos // 4, pos % 4
    xi = gx * 2 + core
    last_x = 2 * lax.axis_size("gx") - 1

    far_gy = (gy + 2) % 4

    def worker(s, c):
        return (gx, far_gy, (((gy + 2 + 4 * s) % 8) // 4) * 2 + c)

    def owner(j):
        return (gx, far_gy, j)

    def place(dx, dy):
        x, d = xi + dx, (chip + dy + 8) % 8
        return (x // 2, d % 4, (d // 4) * 2 + x % 2)

    has_xp, has_xn = xi > 0, xi < last_x
    has_yp, has_yn = blk > 0, blk < 3
    across = (gx, gy, (1 - hi) * 2 + core)

    barrier = pltpu.get_barrier_semaphore()
    neighbours = [
        (has_xp, place(-1, 0)), (has_xn, place(1, 0)), (has_yp, place(0, -1)), (has_yn, place(0, 1)),
        (jnp.logical_and(has_xp, has_yp), place(-1, -1)), (jnp.logical_and(has_xn, has_yn), place(1, 1)),
    ]
    for j in range(4):
        pl.semaphore_signal(barrier, inc=1, device_id=owner(j), device_id_type=MESH)
    pl.semaphore_signal(barrier, inc=1, device_id=across, device_id_type=MESH)
    for cond, dev in neighbours:
        @pl.when(cond)
        def _():
            pl.semaphore_signal(barrier, inc=1, device_id=dev, device_id_type=MESH)

    pairs = (
        (field_in, field), (var_in, var), (mean_in, mean), (source_in, source), (cols_in, cols), (vals_in, vals),
    )
    staged = [pltpu.make_async_copy(a, b, loads.at[i]) for i, (a, b) in enumerate(pairs)]
    for op in staged:
        op.start()

    keep = (lax.broadcasted_iota(jnp.int32, (16, 128), 0) + SL * ch < P_SIZE)
    keep_tail = SL * ch + 16 < P_SIZE
    low16, low8 = lanes(16) < 64, lanes(8) < 64

    def tails(t):
        r = pltpu.roll(swing(t), 4, 0)
        return jnp.where(low8, t, r), swing(jnp.where(low8, r, t))

    def pack(ref, out):
        for x in range(4):
            c, xl = x // 2, x % 2
            for y in range(4):
                v = xl * 4 + y
                a = jnp.where(keep, ref[pl.ds(x * 8 + y, 16, stride=32), :], 0.0)
                b = swing(jnp.where(keep, ref[pl.ds(x * 8 + y + 4, 16, stride=32), :], 0.0))
                out[pl.ds(c * OWN + v * 16, 16), :] = jnp.where(low16, a, b)
                out[pl.ds((2 + c) * OWN + v * 16, 16), :] = swing(jnp.where(low16, b, a))
            ta, tb = tails(jnp.where(keep_tail, ref[pl.ds(512 + x * 8, 8), :], 0.0))
            out[pl.ds(c * OWN + 128 + xl * 4, 4), :] = ta[0:4]
            out[pl.ds((2 + c) * OWN + 128 + xl * 4, 4), :] = tb[0:4]

    def piece(ref, i):
        return ref.at[pl.ds(pl.multiple_of(i * OWN, 8), OWN), :]

    def copy(src, dst, k, l, dev):
        return pltpu.make_async_remote_copy(
            src_ref=src, dst_ref=dst, send_sem=send.at[k], recv_sem=recv.at[l], device_id=dev, device_id_type=MESH
        )

    staged[0].wait()
    pack(field, fs)
    pl.semaphore_wait(barrier, 5 + sum(jnp.where(cond, 1, 0) for cond, dev in neighbours))

    for c in range(2):
        for s in range(2):
            copy(piece(fs, 2 * s + c), piece(fr, ch), 2 * s + c, ch, worker(s, c)).start()

    staged[1].wait()
    staged[2].wait()
    for k in range(TERMS + 1):
        for xl in range(2):
            if k < TERMS:
                t = var[pl.ds(pl.multiple_of(k * 32 + core * 16 + xl * 8, 8), 8), :]
            else:
                t = mean[pl.ds(pl.multiple_of(core * 16 + xl * 8, 8), 8), :]
            ta, tb = tails(t)
            cs[pl.ds(k * 8 + xl * 4, 4), :] = jnp.where(hi == 0, ta, tb)[0:4]
    coefs = copy(cs, cr, 8, 8, worker(hi, core))
    coefs.start()

    staged[3].wait()
    pack(source, ss)
    for c in range(2):
        for s in range(2):
            copy(piece(ss, 2 * s + c), piece(sr, ch), 4 + 2 * s + c, 4 + ch, worker(s, c)).start()

    zero_vec = jnp.zeros((VEC, 128), F32)
    for cond, xref, yref in ((xi == 0, (xlo1, xlo2), ()), (xi == last_x, (xhi1, xhi2), ()),
                             (blk == 0, (), (ylo1, ylo2)), (blk == 3, (), (yhi1, yhi2))):
        @pl.when(cond)
        def _():
            for ref in xref:
                for i in range(4):
                    ref[pl.ds(i * VEC, VEC), :] = zero_vec
            for ref in yref:
                ref[...] = zero_vec

    @pl.when(xi == 0)
    def _():
        cxr[...] = jnp.zeros((2 * VEC, 128), F32)

    @pl.when(blk == 0)
    def _():
        cyr[...] = zero_vec

    @pl.when(jnp.logical_or(xi == 0, blk == 0))
    def _():
        cxyr[...] = zero_vec

    lane72 = lanes(VEC)
    low = lane72 < 64
    z64 = jnp.bitwise_and(lane72, 63)
    edge = 63 * (1 - side)
    edge_lane = z64 == edge
    first_lane, end_lane = z64 == 0, z64 == 63

    def vec(ref, v):
        return ref[pl.ds(v * VEC, VEC), :]

    def gather(src, dst):
        for v in range(8):
            for j in range(4):
                dst[pl.ds(v * VEC + 16 * j, 16), :] = src[pl.ds(j * OWN + 16 * v, 16), :]
            dst[pl.ds(v * VEC + 64, 4), :] = src[pl.ds(128 + v, 4, stride=OWN), :]
            dst[pl.ds(v * VEC + 68, 4), :] = jnp.zeros((4, 128), F32)

    def arrived(dst, k, l):
        copy(dst, dst, k, l, across).wait_recv()

    def spread(val, stage, halos, base):
        xlo, xhi, ylo, yhi, z, zfull = halos
        up = stage.at[pl.ds(0, VEC), :]
        down = stage.at[pl.ds(VEC, VEC), :]
        zs = stage.at[pl.ds(2 * VEC, 16), :]
        xn = copy(val.at[pl.ds(4 * VEC, 4 * VEC), :], xlo, base, base, place(1, 0))
        xp = copy(val.at[pl.ds(0, 4 * VEC), :], xhi, base + 1, base + 1, place(-1, 0))
        yn = copy(up, ylo, base + 2, base + 2, place(0, 1))
        yp = copy(down, yhi, base + 3, base + 3, place(0, -1))
        zc = copy(zs, z, base + 4, base + 4, across)

        total = zero_vec
        for v in range(8):
            total = jnp.where(z64 == v, pltpu.roll(vec(val, v), v + 65 * (1 - side), 1), total)
        for t in range(8):
            part = total[8 * t:8 * t + 8]
            packed = jnp.where(z64[0:8] // 8 == t, pltpu.roll(part, 8 * t, 1) if t else part, packed) if t else part
        stage[pl.ds(2 * VEC, 8), :] = packed
        stage[pl.ds(2 * VEC + 8, 8), :] = total[64:72]
        zc.start()

        @pl.when(has_xn)
        def _():
            xn.start()

        @pl.when(has_xp)
        def _():
            xp.start()

        up[...] = jnp.where(low, swing(vec(val, 3)), vec(val, 7))
        down[...] = jnp.where(low, vec(val, 0), swing(vec(val, 4)))

        @pl.when(has_yn)
        def _():
            yn.start()

        @pl.when(has_yp)
        def _():
            yp.start()

        return xn, xp, yn, yp, zc

    def collect(ops):
        xn, xp, yn, yp, zc = ops

        @pl.when(has_xp)
        def _():
            xn.wait_recv()

        @pl.when(has_xn)
        def _():
            xp.wait_recv()

        @pl.when(has_yp)
        def _():
            yn.wait_recv()

        @pl.when(has_yn)
        def _():
            yp.wait_recv()

        zc.wait_recv()

    def laplace(val, halos):
        xlo, xhi, ylo, yhi, zpacked, z = halos
        for t in range(8):
            z[pl.ds(8 * t, 8), :] = pltpu.roll(zpacked[0:8, :], (128 - 8 * t) % 128, 1) if t else zpacked[0:8, :]
        z[pl.ds(64, 8), :] = zpacked[8:16, :]
        for x in range(2):
            for y in range(4):
                v = 4 * x + y
                here = vec(val, v)
                beside = (vec(val, v - 4) if x else vec(xlo, y)) + (vec(xhi, y) if x else vec(val, v + 4))
                if y > 0:
                    beside = beside + vec(val, v - 1)
                elif x == 0:
                    beside = beside + jnp.where(low, ylo[...], swing(vec(val, 3)))
                else:
                    beside = beside + swing(jnp.where(low, vec(val, 7), ylo[...]))
                if y < 3:
                    beside = beside + vec(val, v + 1)
                elif x == 0:
                    beside = beside + swing(jnp.where(low, yhi[...], vec(val, 0)))
                else:
                    beside = beside + jnp.where(low, swing(vec(val, 4)), yhi[...])
                beside = beside + jnp.where(first_lane, 0.0, pltpu.roll(here, 1, 1))
                beside = beside + jnp.where(end_lane, 0.0, pltpu.roll(here, 127, 1))
                beside = beside + jnp.where(edge_lane, pltpu.roll(z[...], (edge + 128 - v) % 128, 1), 0.0)
                out = 6.0 * here - beside
                lap[pl.ds(v * VEC, VEC), :] = out
                b1 = out.astype(BF16)
                b2 = (out - b1.astype(F32)).astype(BF16)
                r, h = (v // 2) * 256, (v % 2) * 128
                rhs[r:r + VEC, h:h + 128] = b1
                rhs[r + KSEG:r + KSEG + VEC, h:h + 128] = b2
                rhs[r + 2 * KSEG:r + 2 * KSEG + VEC, h:h + 128] = b1

    def operate(use):
        def step(q, carry):
            mixed = jnp.dot(
                left16[...], rhs[pl.ds(pl.multiple_of(q * 256, 256), 256), :], preferred_element_type=F32
            )
            for h in range(2):
                v = 2 * q + h
                rows = pl.ds(pl.multiple_of(v * VEC, 8), VEC)
                m = cr[pl.ds(TERMS * 8 + v, 1), :]
                total = m * lap[rows, :]
                for k in range(TERMS):
                    total = total + cr[pl.ds(k * 8 + v, 1), :] * mixed[k * VEC:(k + 1) * VEC, h * 128:(h + 1) * 128]
                use(rows, m, total)
            return carry

        lax.fori_loop(0, 4, step, 0)

    for j in range(4):
        arrived(piece(fr, j), j, j)
    gather(fr, v1)
    halos1 = (xlo1, xhi1, ylo1, yhi1, z1, zfull)
    ops1 = spread(v1, ysend1, halos1, 9)
    rhs[...] = jnp.zeros((4 * 256, 256), BF16)
    gt[...] = jnp.zeros((128, 128), F32)
    staged[4].wait()
    staged[5].wait()
    p = lax.broadcasted_iota(jnp.int32, (KSEG, 68), 0)
    slot = jnp.where(p < 64, SL * lax.shift_right_logical(p, 4) + jnp.bitwise_and(p, 15),
                     jnp.where(p < 68, SL * (p - 64) + 16, -1))
    used = lax.broadcasted_iota(jnp.int32, (1, 68), 1) < P_SIZE

    def build(k, carry):
        total = jnp.zeros((KSEG, 68), F32)
        for b in range(3):
            total = total + jnp.where(slot == cols[k, b:b + 1, :], jnp.where(used, vals[k, b:b + 1, :], 0.0), 0.0)
        gt[0:KSEG, 0:68] = total
        gt2[...] = jnp.transpose(gt[...])
        rows = [gt2[pl.ds(SL * j, 16), :] for j in range(4)]
        rows.append(gt2[pl.ds(16, 4, stride=SL), :])
        rows.append(jnp.zeros((4, 128), F32))
        g = jnp.concatenate(rows, 0)
        a1 = g.astype(BF16).astype(F32)
        a2 = g - a1
        r = pltpu.roll(a1, KSEG, 1)
        left[pl.ds(pl.multiple_of(k * VEC, 8), VEC), 0:128] = jnp.where(lane72 < 80, a1, r)
        left[pl.ds(pl.multiple_of(k * VEC, 8), VEC), 128:256] = jnp.where(lane72 < 32, r, pltpu.roll(a2, 32, 1))
        return carry

    lax.fori_loop(0, TERMS, build, 0)
    left16[...] = left[...].astype(BF16)

    arrived(cr, 8, 8)
    collect(ops1)
    laplace(v1, halos1)
    for j in range(4):
        arrived(piece(sr, j), 4 + j, 4 + j)
    gather(sr, srcv)

    def relax(rows, m, total):
        first = srcv[rows, :] - total
        v2[rows, :] = v1[rows, :] + (2.0 / 3.0) * first / (6.0 * m)

    operate(relax)

    halos2 = (xlo2, xhi2, ylo2, yhi2, z2, zfull)
    ops2 = spread(v2, ysend2, halos2, 14)
    for j in range(4):
        for v in range(8):
            bs[pl.ds(j * OWN + 16 * v, 16), :] = v2[pl.ds(v * VEC + 16 * j, 16), :]
        bs[pl.ds(j * OWN + 128, 8), :] = v2[pl.ds(64 + j, 8, stride=VEC), :]
    here = 2 * side + core
    for j in range(4):
        copy(piece(bs, j), piece(br, here), 19 + j, 19 + here, owner(j)).start()
    row = lax.broadcasted_iota(jnp.int32, (256, 256), 0)
    col = lax.broadcasted_iota(jnp.int32, (256, 256), 1)
    half = jnp.bitwise_and(lax.shift_right_logical(row, 6), 1)
    b_row = 2 * half + lax.shift_right_logical(row, 7)
    z_row = jnp.bitwise_and(row, 63)
    off = z_row - 2 * jnp.bitwise_and(col, 31)
    near = jnp.where(off == 0, 0.5, jnp.where(jnp.logical_or(off == 1, off == -1), 0.25, 0.0))
    main_w = jnp.where(jnp.logical_and(col < 128, lax.shift_right_logical(col, 5) == b_row), near, 0.0)
    next_w = jnp.where(jnp.logical_and(col == 128 + b_row, z_row == 63), 0.25, 0.0)
    wz[...] = (main_w + next_w).astype(BF16)

    collect(ops2)
    laplace(v2, halos2)

    def residual(rows, m, total):
        after[rows, :] = srcv[rows, :] - total

    operate(residual)

    for i in range(2):
        if i == 0:
            c = [0.5 * vec(after, y) + 0.25 * vec(after, 4 + y) for y in range(4)]
        else:
            c = [0.25 * vec(after, 4 + y) for y in range(4)]
        s3 = 0.25 * swing(c[3])
        d0 = 0.5 * c[0] + 0.25 * c[1] + jnp.where(low, 0.0, s3)
        d1 = 0.5 * c[2] + 0.25 * (c[3] + c[1])
        dn = jnp.where(low, s3, 0.0)
        for r, (da, db) in ((i, (d0, d1)), (2 + i, (dn, None))):
            for h, d in ((0, da), (1, db)):
                if d is None:
                    d = zero_vec
                dh = d.astype(BF16)
                dbuf[pl.ds(r * VEC, VEC), h * 128:(h + 1) * 128] = dh.astype(F32)
                dbuf[pl.ds((4 + r) * VEC, VEC), h * 128:(h + 1) * 128] = d - dh.astype(F32)
    parts = jnp.dot(dbuf[...].astype(BF16), wz[...], preferred_element_type=F32)
    parts = parts[0:4 * VEC] + parts[4 * VEC:8 * VEC]

    def both(r):
        return parts[r * VEC:(r + 1) * VEC, 0:128], parts[r * VEC:(r + 1) * VEC, 128:256]

    def one(r):
        a, b = both(r)
        return a + pltpu.roll(b, 32, 1)

    a, b = both(1)
    cxs[0:VEC, :] = a
    cxs[VEC:2 * VEC, :] = b
    cx = copy(cxs, cxr, 23, 23, place(1, 0))

    @pl.when(has_xn)
    def _():
        cx.start()

    cys[0:VEC, :] = one(2)
    cys[VEC:2 * VEC, :] = one(3)
    cy = copy(cys.at[pl.ds(0, VEC), :], cyr, 24, 24, place(0, 1))
    cxy = copy(cys.at[pl.ds(VEC, VEC), :], cxyr, 25, 25, place(1, 1))

    @pl.when(has_yn)
    def _():
        cy.start()

    @pl.when(jnp.logical_and(has_xn, has_yn))
    def _():
        cxy.start()

    for j in range(4):
        arrived(piece(br, j), 19 + j, 19 + j)
    for x in range(4):
        c, xl = x // 2, x % 2
        for y in range(4):
            v = 4 * xl + y
            va = br[pl.ds(c * OWN + 16 * v, 16), :]
            vb = br[pl.ds((2 + c) * OWN + 16 * v, 16), :]
            smoothed[pl.ds(x * 8 + y, 16, stride=32), :] = jnp.where(low16, va, swing(vb))
            smoothed[pl.ds(x * 8 + y + 4, 16, stride=32), :] = jnp.where(low16, swing(va), vb)
        ta = br[pl.ds(c * OWN + 128, 8), :]
        tb = br[pl.ds((2 + c) * OWN + 128, 8), :]
        smoothed[pl.ds(512 + x * 8, 4), :] = jnp.where(low8, ta, swing(tb))[4 * xl:4 * xl + 4]
        smoothed[pl.ds(512 + x * 8 + 4, 4), :] = jnp.where(low8, swing(ta), tb)[4 * xl:4 * xl + 4]

    a, b = both(0)

    @pl.when(has_xp)
    def _():
        cx.wait_recv()

    @pl.when(has_yp)
    def _():
        cy.wait_recv()

    @pl.when(jnp.logical_and(has_xp, has_yp))
    def _():
        cxy.wait_recv()

    ysum = cyr[...] + cxyr[...]
    fin[0:VEC, :] = a + cxr[0:VEC, :] + jnp.where(lane72 < 32, ysum, 0.0)
    fin[VEC:2 * VEC, :] = b + cxr[VEC:2 * VEC, :] + jnp.where(lane72 == 0, pltpu.roll(ysum, 96, 1), 0.0)
    for j in range(4):
        cbs[pl.ds(j * 40, 16), :] = fin[pl.ds(16 * j, 16), :]
        cbs[pl.ds(j * 40 + 16, 16), :] = fin[pl.ds(VEC + 16 * j, 16), :]
        cbs[pl.ds(j * 40 + 32, 2), :] = fin[pl.ds(64 + j, 2, stride=VEC), :]
        cbs[pl.ds(j * 40 + 34, 6), :] = jnp.zeros((6, 128), F32)

    def small(ref, i):
        return ref.at[pl.ds(pl.multiple_of(i * 40, 8), 40), :]

    for j in range(4):
        copy(small(cbs, j), small(cbr, here), 26 + j, 26 + here, owner(j)).start()
    for j in range(4):
        arrived(small(cbr, j), 26 + j, 26 + j)
    lane16 = lanes(16)
    for x in range(2):
        ma, mb = cbr[pl.ds(x * 40, 16), :], cbr[pl.ds((2 + x) * 40, 16), :]
        za = cbr[pl.ds(x * 40 + 16, 16), :]
        tl, tr = cbr[pl.ds(x * 40 + 32, 8), :], cbr[pl.ds((2 + x) * 40 + 32, 8), :]
        for b in range(4):
            def joined(left_, right_, extra, lane):
                out = jnp.where(lane < 32, pltpu.roll(left_, (128 - 32 * b) % 128, 1), pltpu.roll(right_, (160 - 32 * b) % 128, 1))
                return out + jnp.where(lane == 32, pltpu.roll(extra, 32 - b, 1), 0.0)

            coarse[pl.ds(x * 4 + b, 16, stride=8), :] = joined(ma, mb, za, lane16)
            t = joined(tl, tr, pltpu.roll(tl, 7, 0), lanes(8))
            coarse[pl.ds(128 + x * 4 + b, 1), :] = t[0:1]

    for j in range(4):
        copy(piece(fs, j), piece(fr, j), j, j, across).wait_send()
        copy(piece(ss, j), piece(sr, j), 4 + j, 4 + j, across).wait_send()
        copy(piece(bs, j), piece(br, j), 19 + j, 19 + j, across).wait_send()
        copy(small(cbs, j), small(cbr, j), 26 + j, 26 + j, across).wait_send()
    coefs.wait_send()
    for xn, xp, yn, yp, zc in (ops1, ops2):
        zc.wait_send()
        for cond, op in ((has_xn, xn), (has_xp, xp), (has_yn, yn), (has_yp, yp)):
            @pl.when(cond)
            def _():
                op.wait_send()
    for cond, op in ((has_xn, cx), (has_yn, cy), (jnp.logical_and(has_xn, has_yn), cxy)):
        @pl.when(cond)
        def _():
            op.wait_send()


def scratch():
    def rows(n, width=128, kind=F32):
        return pltpu.VMEM((n, width), kind)

    halos = [rows(4 * VEC), rows(4 * VEC), rows(VEC), rows(VEC), rows(16)]
    return [
        rows(SL * 32), rows(SL * 32), rows(32), rows(TERMS * 32), pltpu.VMEM((TERMS, 3, 4 * SL), jnp.int32),
        pltpu.VMEM((TERMS, 3, 4 * SL), F32), pltpu.SemaphoreType.DMA((6,)),
        rows(4 * OWN), rows(4 * OWN), rows(8 * (TERMS + 1)), rows(4 * OWN), rows(4 * OWN), rows(8 * (TERMS + 1)),
        rows(ALL), rows(ALL), *halos, *halos, rows(VEC), rows(2 * VEC + 16), rows(2 * VEC + 16), rows(ALL), rows(4 * 256, 256, BF16),
        rows(TERMS * VEC, 256), rows(TERMS * VEC, 256, BF16), rows(128), rows(128), rows(ALL), rows(ALL), rows(256, 256, BF16),
        rows(4 * OWN), rows(4 * OWN), rows(8 * VEC, 256), rows(2 * VEC), rows(2 * VEC), rows(2 * VEC), rows(VEC),
        rows(VEC), rows(2 * VEC), rows(160), rows(160),
        pltpu.SemaphoreType.DMA((30,)), pltpu.SemaphoreType.DMA((30,)),
    ]


def body(field, source, mean_coef, var_coefs, galerkin_cols, galerkin_vals):
    whole = pl.BlockSpec(memory_space=pltpu.VMEM)
    smoothed, coarse = pl.pallas_call(
        kernel,
        out_shape=(jax.ShapeDtypeStruct((SL * 32, 128), F32), jax.ShapeDtypeStruct((SL * 8, 128), F32)),
        in_specs=[pl.BlockSpec(memory_space=pl.ANY)] * 6,
        out_specs=(whole, whole),
        scratch_shapes=scratch(),
        compiler_params=pltpu.CompilerParams(collective_id=0, has_side_effects=True),
        name="sweep",
    )(
        field.reshape(SL * 32, 128), source.reshape(SL * 32, 128), mean_coef.reshape(32, 128),
        var_coefs.reshape(TERMS * 32, 128), jnp.swapaxes(galerkin_cols, 1, 2), jnp.swapaxes(galerkin_vals, 1, 2),
    )
    return smoothed.reshape(field.shape), coarse[:, 0:64].reshape(SL, 2, 4, 64)


def solution(mesh):
    wide = P("chaos", "gx", "gy", None)
    return jax.shard_map(
        body,
        mesh=mesh,
        in_specs=(wide, wide, P("gx", "gy", None), P(None, "gx", "gy", None), P(), P()),
        out_specs=(wide, wide),
        check_vma=False,
    )
```

```python
import jax
import jax.numpy as jnp
from jax import lax
from jax.experimental import pallas as pl
from jax.experimental.pallas import tpu as pltpu
from jax.sharding import PartitionSpec as P


P_SIZE = 66
MESH = pl.DeviceIdType.MESH
SL = 17
OWN = 136
VEC = 72
ALL = 8 * VEC
TERMS = 10
KSEG = 80
F32 = jnp.float32
BF16 = jnp.bfloat16


def lanes(rows):
    return lax.broadcasted_iota(jnp.int32, (rows, 128), 1)


def swing(a):
    return pltpu.roll(a, 64, 1)


def kernel(
    field_in, source_in, mean_in, var_in, cols_in, vals_in, smoothed, coarse,
    field, source, mean, var, cols, vals, loads,
    fs, ss, cs, fr, sr, cr, v1, v2, xlo1, xhi1, ylo1, yhi1, z1, xlo2, xhi2, ylo2, yhi2, z2, zfull,
    ysend1, ysend2, lap, rhs, left, left16, gt, gt2, srcv, after, wz, bs, br, dbuf, cms, cxs, cys, cxys, cmr, cxr, cyr, cxyr,
    send, recv,
):
    gx, gy, ch = lax.axis_index("gx"), lax.axis_index("gy"), lax.axis_index("chaos")
    hi, core = ch // 2, ch % 2
    chip = hi * 4 + gy
    pos = (chip + 6) % 8
    side, blk = pos // 4, pos % 4
    xi = gx * 2 + core
    last_x = 2 * lax.axis_size("gx") - 1

    far_gy = (gy + 2) % 4

    def worker(s, c):
        return (gx, far_gy, (((gy + 2 + 4 * s) % 8) // 4) * 2 + c)

    def owner(j):
        return (gx, far_gy, j)

    def place(dx, dy):
        x, d = xi + dx, (chip + dy + 8) % 8
        return (x // 2, d % 4, (d // 4) * 2 + x % 2)

    has_xp, has_xn = xi > 0, xi < last_x
    has_yp, has_yn = blk > 0, blk < 3
    across = (gx, gy, (1 - hi) * 2 + core)

    barrier = pltpu.get_barrier_semaphore()
    neighbours = [
        (has_xp, place(-1, 0)), (has_xn, place(1, 0)), (has_yp, place(0, -1)), (has_yn, place(0, 1)),
    ]
    more_y, more_x = gy > 0, gx > 0
    for s in range(2):
        lower = ((gy + 1 + 4 * s) % 8) // 4 * 2
        for c in range(2):
            neighbours.append((more_y, (gx, (gy + 1) % 4, lower + c)))
        neighbours.append((more_x, (gx - 1, far_gy, worker(s, 1)[2])))
        neighbours.append((jnp.logical_and(more_x, more_y), (gx - 1, (gy + 1) % 4, lower + 1)))
    for j in range(4):
        pl.semaphore_signal(barrier, inc=1, device_id=owner(j), device_id_type=MESH)
    pl.semaphore_signal(barrier, inc=1, device_id=across, device_id_type=MESH)
    for cond, dev in neighbours:
        @pl.when(cond)
        def _():
            pl.semaphore_signal(barrier, inc=1, device_id=dev, device_id_type=MESH)

    pairs = (
        (field_in, field), (var_in, var), (mean_in, mean), (source_in, source), (cols_in, cols), (vals_in, vals),
    )
    staged = [pltpu.make_async_copy(a, b, loads.at[i]) for i, (a, b) in enumerate(pairs)]
    for op in staged:
        op.start()

    keep = (lax.broadcasted_iota(jnp.int32, (16, 128), 0) + SL * ch < P_SIZE)
    keep_tail = SL * ch + 16 < P_SIZE
    low16, low8 = lanes(16) < 64, lanes(8) < 64

    def tails(t):
        r = pltpu.roll(swing(t), 4, 0)
        return jnp.where(low8, t, r), swing(jnp.where(low8, r, t))

    def pack(ref, out):
        for x in range(4):
            c, xl = x // 2, x % 2
            for y in range(4):
                v = xl * 4 + y
                a = jnp.where(keep, ref[pl.ds(x * 8 + y, 16, stride=32), :], 0.0)
                b = swing(jnp.where(keep, ref[pl.ds(x * 8 + y + 4, 16, stride=32), :], 0.0))
                out[pl.ds(c * OWN + v * 16, 16), :] = jnp.where(low16, a, b)
                out[pl.ds((2 + c) * OWN + v * 16, 16), :] = swing(jnp.where(low16, b, a))
            ta, tb = tails(jnp.where(keep_tail, ref[pl.ds(512 + x * 8, 8), :], 0.0))
            out[pl.ds(c * OWN + 128 + xl * 4, 4), :] = ta[0:4]
            out[pl.ds((2 + c) * OWN + 128 + xl * 4, 4), :] = tb[0:4]

    def piece(ref, i):
        return ref.at[pl.ds(pl.multiple_of(i * OWN, 8), OWN), :]

    def copy(src, dst, k, l, dev):
        return pltpu.make_async_remote_copy(
            src_ref=src, dst_ref=dst, send_sem=send.at[k], recv_sem=recv.at[l], device_id=dev, device_id_type=MESH
        )

    staged[0].wait()
    pack(field, fs)
    pl.semaphore_wait(barrier, 5 + sum(jnp.where(cond, 1, 0) for cond, dev in neighbours[0:4])
                      + jnp.where(has_yn, 4, 0) + 4 * core * jnp.where(has_xn, 1, 0) * jnp.where(has_yn, 2, 1))

    for c in range(2):
        for s in range(2):
            copy(piece(fs, 2 * s + c), piece(fr, ch), 2 * s + c, ch, worker(s, c)).start()

    staged[1].wait()
    staged[2].wait()
    for k in range(TERMS + 1):
        for xl in range(2):
            if k < TERMS:
                t = var[pl.ds(pl.multiple_of(k * 32 + core * 16 + xl * 8, 8), 8), :]
            else:
                t = mean[pl.ds(pl.multiple_of(core * 16 + xl * 8, 8), 8), :]
            ta, tb = tails(t)
            cs[pl.ds(k * 8 + xl * 4, 4), :] = jnp.where(hi == 0, ta, tb)[0:4]
    coefs = copy(cs, cr, 8, 8, worker(hi, core))
    coefs.start()

    staged[3].wait()
    pack(source, ss)
    for c in range(2):
        for s in range(2):
            copy(piece(ss, 2 * s + c), piece(sr, ch), 4 + 2 * s + c, 4 + ch, worker(s, c)).start()

    zero_vec = jnp.zeros((VEC, 128), F32)
    for cond, xref, yref in ((xi == 0, (xlo1, xlo2), ()), (xi == last_x, (xhi1, xhi2), ()),
                             (blk == 0, (), (ylo1, ylo2)), (blk == 3, (), (yhi1, yhi2))):
        @pl.when(cond)
        def _():
            for ref in xref:
                for i in range(4):
                    ref[pl.ds(i * VEC, VEC), :] = zero_vec
            for ref in yref:
                ref[...] = zero_vec

    def clear(ref, n, rows):
        for r in rows:
            ref[pl.ds(r * n, n), :] = jnp.zeros((n, 128), F32)

    @pl.when(gx == 0)
    def _():
        clear(cxr, 32, (0, 2))

    @pl.when(gy == 0)
    def _():
        clear(cyr, 16, range(4))
        clear(cxyr, 16, range(4))

    @pl.when(jnp.logical_and(gx == 0, gy > 0))
    def _():
        clear(cxyr, 16, (0, 2))

    clear(cms, 32, range(4))
    clear(cxs, 32, range(4))
    clear(cys, 16, range(4))
    clear(cxys, 16, range(4))

    lane72 = lanes(VEC)
    low = lane72 < 64
    z64 = jnp.bitwise_and(lane72, 63)
    edge = 63 * (1 - side)
    edge_lane = z64 == edge
    first_lane, end_lane = z64 == 0, z64 == 63

    def vec(ref, v):
        return ref[pl.ds(v * VEC, VEC), :]

    def gather(src, dst):
        for v in range(8):
            for j in range(4):
                dst[pl.ds(v * VEC + 16 * j, 16), :] = src[pl.ds(j * OWN + 16 * v, 16), :]
            dst[pl.ds(v * VEC + 64, 4), :] = src[pl.ds(128 + v, 4, stride=OWN), :]
            dst[pl.ds(v * VEC + 68, 4), :] = jnp.zeros((4, 128), F32)

    def arrived(dst, k, l):
        copy(dst, dst, k, l, across).wait_recv()

    def spread(val, stage, halos, base):
        xlo, xhi, ylo, yhi, z, zfull = halos
        up = stage.at[pl.ds(0, VEC), :]
        down = stage.at[pl.ds(VEC, VEC), :]
        zs = stage.at[pl.ds(2 * VEC, 16), :]
        xn = copy(val.at[pl.ds(4 * VEC, 4 * VEC), :], xlo, base, base, place(1, 0))
        xp = copy(val.at[pl.ds(0, 4 * VEC), :], xhi, base + 1, base + 1, place(-1, 0))
        yn = copy(up, ylo, base + 2, base + 2, place(0, 1))
        yp = copy(down, yhi, base + 3, base + 3, place(0, -1))
        zc = copy(zs, z, base + 4, base + 4, across)

        @pl.when(has_xn)
        def _():
            xn.start()

        @pl.when(has_xp)
        def _():
            xp.start()

        total = zero_vec
        for v in range(8):
            total = jnp.where(z64 == v, pltpu.roll(vec(val, v), v + 65 * (1 - side), 1), total)
        for t in range(8):
            part = total[8 * t:8 * t + 8]
            packed = jnp.where(z64[0:8] // 8 == t, pltpu.roll(part, 8 * t, 1) if t else part, packed) if t else part
        stage[pl.ds(2 * VEC, 8), :] = packed
        stage[pl.ds(2 * VEC + 8, 8), :] = total[64:72]
        zc.start()

        up[...] = jnp.where(low, swing(vec(val, 3)), vec(val, 7))
        down[...] = jnp.where(low, vec(val, 0), swing(vec(val, 4)))

        @pl.when(has_yn)
        def _():
            yn.start()

        @pl.when(has_yp)
        def _():
            yp.start()

        return xn, xp, yn, yp, zc

    def collect(ops):
        xn, xp, yn, yp, zc = ops

        @pl.when(has_xp)
        def _():
            xn.wait_recv()

        @pl.when(has_xn)
        def _():
            xp.wait_recv()

        @pl.when(has_yp)
        def _():
            yn.wait_recv()

        @pl.when(has_yn)
        def _():
            yp.wait_recv()

        zc.wait_recv()

    def laplace(val, halos):
        xlo, xhi, ylo, yhi, zpacked, z = halos
        for t in range(8):
            z[pl.ds(8 * t, 8), :] = pltpu.roll(zpacked[0:8, :], (128 - 8 * t) % 128, 1) if t else zpacked[0:8, :]
        z[pl.ds(64, 8), :] = zpacked[8:16, :]
        for x in range(2):
            for y in range(4):
                v = 4 * x + y
                here = vec(val, v)
                beside = (vec(val, v - 4) if x else vec(xlo, y)) + (vec(xhi, y) if x else vec(val, v + 4))
                if y > 0:
                    beside = beside + vec(val, v - 1)
                elif x == 0:
                    beside = beside + jnp.where(low, ylo[...], swing(vec(val, 3)))
                else:
                    beside = beside + swing(jnp.where(low, vec(val, 7), ylo[...]))
                if y < 3:
                    beside = beside + vec(val, v + 1)
                elif x == 0:
                    beside = beside + swing(jnp.where(low, yhi[...], vec(val, 0)))
                else:
                    beside = beside + jnp.where(low, swing(vec(val, 4)), yhi[...])
                beside = beside + jnp.where(first_lane, 0.0, pltpu.roll(here, 1, 1))
                beside = beside + jnp.where(end_lane, 0.0, pltpu.roll(here, 127, 1))
                beside = beside + jnp.where(edge_lane, pltpu.roll(z[...], (edge + 128 - v) % 128, 1), 0.0)
                out = 6.0 * here - beside
                lap[pl.ds(v * VEC, VEC), :] = out
                b1 = out.astype(BF16)
                b2 = (out - b1.astype(F32)).astype(BF16)
                r, h = (v // 2) * 256, (v % 2) * 128
                rhs[r:r + VEC, h:h + 128] = b1
                rhs[r + KSEG:r + KSEG + VEC, h:h + 128] = b2
                rhs[r + 2 * KSEG:r + 2 * KSEG + VEC, h:h + 128] = b1

    def operate(use):
        def step(q, carry):
            mixed = jnp.dot(
                left16[...], rhs[pl.ds(pl.multiple_of(q * 256, 256), 256), :], preferred_element_type=F32
            )
            for h in range(2):
                v = 2 * q + h
                rows = pl.ds(pl.multiple_of(v * VEC, 8), VEC)
                m = cr[pl.ds(TERMS * 8 + v, 1), :]
                total = m * lap[rows, :]
                for k in range(TERMS):
                    total = total + cr[pl.ds(k * 8 + v, 1), :] * mixed[k * VEC:(k + 1) * VEC, h * 128:(h + 1) * 128]
                use(rows, m, total)
            return carry

        lax.fori_loop(0, 4, step, 0)

    for j in range(4):
        arrived(piece(fr, j), j, j)
    gather(fr, v1)
    halos1 = (xlo1, xhi1, ylo1, yhi1, z1, zfull)
    ops1 = spread(v1, ysend1, halos1, 9)
    rhs[...] = jnp.zeros((4 * 256, 256), BF16)
    gt[...] = jnp.zeros((128, 128), F32)
    staged[4].wait()
    staged[5].wait()
    p = lax.broadcasted_iota(jnp.int32, (KSEG, 68), 0)
    slot = jnp.where(p < 64, SL * lax.shift_right_logical(p, 4) + jnp.bitwise_and(p, 15),
                     jnp.where(p < 68, SL * (p - 64) + 16, -1))
    used = lax.broadcasted_iota(jnp.int32, (1, 68), 1) < P_SIZE

    def build(k, carry):
        total = jnp.zeros((KSEG, 68), F32)
        for b in range(3):
            total = total + jnp.where(slot == cols[k, b:b + 1, :], jnp.where(used, vals[k, b:b + 1, :], 0.0), 0.0)
        gt[0:KSEG, 0:68] = total
        gt2[...] = jnp.transpose(gt[...])
        rows = [gt2[pl.ds(SL * j, 16), :] for j in range(4)]
        rows.append(gt2[pl.ds(16, 4, stride=SL), :])
        rows.append(jnp.zeros((4, 128), F32))
        g = jnp.concatenate(rows, 0)
        a1 = g.astype(BF16).astype(F32)
        a2 = g - a1
        r = pltpu.roll(a1, KSEG, 1)
        left[pl.ds(pl.multiple_of(k * VEC, 8), VEC), 0:128] = jnp.where(lane72 < 80, a1, r)
        left[pl.ds(pl.multiple_of(k * VEC, 8), VEC), 128:256] = jnp.where(lane72 < 32, r, pltpu.roll(a2, 32, 1))
        return carry

    lax.fori_loop(0, TERMS, build, 0)
    left16[...] = left[...].astype(BF16)

    arrived(cr, 8, 8)
    collect(ops1)
    laplace(v1, halos1)
    for j in range(4):
        arrived(piece(sr, j), 4 + j, 4 + j)
    gather(sr, srcv)

    def relax(rows, m, total):
        first = srcv[rows, :] - total
        v2[rows, :] = v1[rows, :] + (2.0 / 3.0) * first / (6.0 * m)

    operate(relax)

    halos2 = (xlo2, xhi2, ylo2, yhi2, z2, zfull)
    ops2 = spread(v2, ysend2, halos2, 14)
    for j in range(4):
        for v in range(8):
            bs[pl.ds(j * OWN + 16 * v, 16), :] = v2[pl.ds(v * VEC + 16 * j, 16), :]
        bs[pl.ds(j * OWN + 128, 8), :] = v2[pl.ds(64 + j, 8, stride=VEC), :]
    here = 2 * side + core
    for j in range(4):
        copy(piece(bs, j), piece(br, here), 19 + j, 19 + here, owner(j)).start()
    row = lax.broadcasted_iota(jnp.int32, (256, 256), 0)
    col = lax.broadcasted_iota(jnp.int32, (256, 256), 1)
    half = jnp.bitwise_and(lax.shift_right_logical(row, 6), 1)
    b_row = 2 * half + lax.shift_right_logical(row, 7)
    z_row = jnp.bitwise_and(row, 63)
    off = z_row - 2 * jnp.bitwise_and(col, 31)
    near = jnp.where(off == 0, 0.5, jnp.where(jnp.logical_or(off == 1, off == -1), 0.25, 0.0))
    main_w = jnp.where(jnp.logical_and(col < 128, lax.shift_right_logical(col, 5) == b_row), near, 0.0)
    next_w = jnp.where(jnp.logical_and(col == 128 + b_row, z_row == 63), 0.25, 0.0)
    wz[...] = (main_w + next_w).astype(BF16)

    collect(ops2)
    laplace(v2, halos2)

    def residual(rows, m, total):
        after[rows, :] = srcv[rows, :] - total

    operate(residual)

    for i in range(2):
        if i == 0:
            c = [0.5 * vec(after, y) + 0.25 * vec(after, 4 + y) for y in range(4)]
        else:
            c = [0.25 * vec(after, 4 + y) for y in range(4)]
        s3 = 0.25 * swing(c[3])
        d0 = 0.5 * c[0] + 0.25 * c[1] + jnp.where(low, 0.0, s3)
        d1 = 0.5 * c[2] + 0.25 * (c[3] + c[1])
        dn = jnp.where(low, s3, 0.0)
        for r, (da, db) in ((i, (d0, d1)), (2 + i, (dn, None))):
            for h, d in ((0, da), (1, db)):
                if d is None:
                    d = zero_vec
                dh = d.astype(BF16)
                dbuf[pl.ds(r * VEC, VEC), h * 128:(h + 1) * 128] = dh.astype(F32)
                dbuf[pl.ds((4 + r) * VEC, VEC), h * 128:(h + 1) * 128] = d - dh.astype(F32)
    parts = jnp.dot(dbuf[...].astype(BF16), wz[...], preferred_element_type=F32)
    parts = parts[0:4 * VEC] + parts[4 * VEC:8 * VEC]

    def both(r):
        return parts[r * VEC:(r + 1) * VEC, 0:128], parts[r * VEC:(r + 1) * VEC, 128:256]

    lane8 = lanes(8)

    def wide(out, r):
        a, b = both(r)
        for j in range(4):
            out[pl.ds(j * 32, 16), :] = a[16 * j:16 * j + 16]
            out[pl.ds(j * 32 + 16, 8), :] = jnp.where(
                lane8 < 8, b[16 * j:16 * j + 8], pltpu.roll(b[16 * j + 8:16 * j + 16], 8, 1)
            )
            out[pl.ds(j * 32 + 24, 1), :] = a[64 + j:65 + j]
            out[pl.ds(j * 32 + 25, 1), :] = b[64 + j:65 + j]

    def slim(out, r):
        a, b = both(r)
        w = a + pltpu.roll(b, 32, 1)
        for j in range(4):
            out[pl.ds(j * 16, 8), :] = w[16 * j:16 * j + 8] + pltpu.roll(w[16 * j + 8:16 * j + 16], 64, 1)
            out[pl.ds(j * 16 + 8, 1), :] = w[64 + j:65 + j]

    def cut(ref, i, n):
        return ref.at[pl.ds(pl.multiple_of(i * n, 8), n), :]

    def parted(src, dst, n, base, slot, dx, dy):
        return [
            copy(cut(src, j, n), cut(dst, slot, n), base + j, base + slot, (gx + dx, far_gy + dy, j)) for j in range(4)
        ]

    there = 2 * side + 1 - core
    has_xyn = jnp.logical_and(has_xn, has_yn)
    results = []
    for fill, r, src, dst, n, base, slot, dx, dy, cond in (
        (wide, 1, cxs, cxr, 32, 30, there, core, 0, has_xn), (slim, 3, cxys, cxyr, 16, 38, there, core, 1, has_xyn),
        (slim, 2, cys, cyr, 16, 34, here, 0, 1, has_yn), (wide, 0, cms, cmr, 32, 26, here, 0, 0, gx >= 0),
    ):
        fill(src, r)
        ops = parted(src, dst, n, base, slot, dx, dy)
        results.append((cond, ops))

        @pl.when(cond)
        def _():
            for op in ops:
                op.start()

    for j in range(4):
        arrived(piece(br, j), 19 + j, 19 + j)
    for x in range(4):
        c, xl = x // 2, x % 2
        for y in range(4):
            v = 4 * xl + y
            va = br[pl.ds(c * OWN + 16 * v, 16), :]
            vb = br[pl.ds((2 + c) * OWN + 16 * v, 16), :]
            smoothed[pl.ds(x * 8 + y, 16, stride=32), :] = jnp.where(low16, va, swing(vb))
            smoothed[pl.ds(x * 8 + y + 4, 16, stride=32), :] = jnp.where(low16, swing(va), vb)
        ta = br[pl.ds(c * OWN + 128, 8), :]
        tb = br[pl.ds((2 + c) * OWN + 128, 8), :]
        smoothed[pl.ds(512 + x * 8, 4), :] = jnp.where(low8, ta, swing(tb))[4 * xl:4 * xl + 4]
        smoothed[pl.ds(512 + x * 8 + 4, 4), :] = jnp.where(low8, swing(ta), tb)[4 * xl:4 * xl + 4]

    for i in range(4):
        arrived(cut(cmr, i, 32), 26, 26 + i)

        @pl.when(more_x if i % 2 == 0 else gx >= 0)
        def _():
            arrived(cut(cxr, i, 32), 30, 30 + i)

        @pl.when(more_y)
        def _():
            arrived(cut(cyr, i, 16), 34, 34 + i)

        @pl.when(jnp.logical_and(more_x, more_y) if i % 2 == 0 else more_y)
        def _():
            arrived(cut(cxyr, i, 16), 38, 38 + i)

    lane16 = lanes(16)

    def unite(i):
        m = cmr[pl.ds(i * 32, 16), :] + cxr[pl.ds(i * 32, 16), :]
        zp = cmr[pl.ds(i * 32 + 16, 8), :] + cxr[pl.ds(i * 32 + 16, 8), :]
        t = cmr[pl.ds(i * 32 + 24, 8), :] + cxr[pl.ds(i * 32 + 24, 8), :]
        yp = cyr[pl.ds(i * 16, 8), :] + cxyr[pl.ds(i * 16, 8), :]
        yt = cyr[pl.ds(i * 16 + 8, 8), :] + cxyr[pl.ds(i * 16 + 8, 8), :]
        z = jnp.concatenate([zp, pltpu.roll(zp, 120, 1)], 0)
        y = jnp.concatenate([yp, swing(yp)], 0)
        m = m + jnp.where(lane16 < 32, y, 0.0)
        return m, z, y, t + jnp.where(lane8 < 32, yt, 0.0), pltpu.roll(t, 7, 0), yt

    for x in range(2):
        ma, za, ya, ta, zt, yt = unite(x)
        mb, _, _, tb, _, _ = unite(2 + x)
        for b in range(4):
            def joined(left_, right_, extra, edge_y, lane):
                out = jnp.where(lane < 32, pltpu.roll(left_, (128 - 32 * b) % 128, 1), pltpu.roll(right_, (160 - 32 * b) % 128, 1))
                extra = pltpu.roll(extra, 32 - b, 1)
                return out + jnp.where(lane == 32, extra + edge_y if b == 0 else extra, 0.0)

            coarse[pl.ds(x * 4 + b, 16, stride=8), :] = joined(ma, mb, za, ya, lane16)
            coarse[pl.ds(128 + x * 4 + b, 1), :] = joined(ta, tb, zt, yt, lane8)[0:1]

    for j in range(4):
        copy(piece(fs, j), piece(fr, j), j, j, across).wait_send()
        copy(piece(ss, j), piece(sr, j), 4 + j, 4 + j, across).wait_send()
        copy(piece(bs, j), piece(br, j), 19 + j, 19 + j, across).wait_send()
    coefs.wait_send()
    for xn, xp, yn, yp, zc in (ops1, ops2):
        zc.wait_send()
        for cond, op in ((has_xn, xn), (has_xp, xp), (has_yn, yn), (has_yp, yp)):
            @pl.when(cond)
            def _():
                op.wait_send()
    for cond, ops in results:
        @pl.when(cond)
        def _():
            for op in ops:
                op.wait_send()


def scratch():
    def rows(n, width=128, kind=F32):
        return pltpu.VMEM((n, width), kind)

    halos = [rows(4 * VEC), rows(4 * VEC), rows(VEC), rows(VEC), rows(16)]
    return [
        rows(SL * 32), rows(SL * 32), rows(32), rows(TERMS * 32), pltpu.VMEM((TERMS, 3, 4 * SL), jnp.int32),
        pltpu.VMEM((TERMS, 3, 4 * SL), F32), pltpu.SemaphoreType.DMA((6,)),
        rows(4 * OWN), rows(4 * OWN), rows(8 * (TERMS + 1)), rows(4 * OWN), rows(4 * OWN), rows(8 * (TERMS + 1)),
        rows(ALL), rows(ALL), *halos, *halos, rows(VEC), rows(2 * VEC + 16), rows(2 * VEC + 16), rows(ALL), rows(4 * 256, 256, BF16),
        rows(TERMS * VEC, 256), rows(TERMS * VEC, 256, BF16), rows(128), rows(128), rows(ALL), rows(ALL), rows(256, 256, BF16),
        rows(4 * OWN), rows(4 * OWN), rows(8 * VEC, 256), rows(128), rows(128), rows(64), rows(64),
        rows(128), rows(128), rows(64), rows(64),
        pltpu.SemaphoreType.DMA((42,)), pltpu.SemaphoreType.DMA((42,)),
    ]


def store(smoothed, coarse, smoothed_out, coarse_out, sems):
    ops = [
        pltpu.make_async_copy(smoothed, smoothed_out, sems.at[0]), pltpu.make_async_copy(coarse, coarse_out, sems.at[1]),
    ]
    for op in ops:
        op.start()
    for op in ops:
        op.wait()


def body(field, source, mean_coef, var_coefs, galerkin_cols, galerkin_vals):
    whole = pl.BlockSpec(memory_space=pltpu.VMEM)
    smoothed, coarse = pl.pallas_call(
        kernel,
        out_shape=(pltpu.VMEM((SL * 32, 128), F32), pltpu.VMEM((SL * 8, 128), F32)),
        in_specs=[pl.BlockSpec(memory_space=pl.ANY)] * 6,
        out_specs=(whole, whole),
        scratch_shapes=scratch(),
        compiler_params=pltpu.CompilerParams(collective_id=0, has_side_effects=True),
        name="sweep",
    )(
        field.reshape(SL * 32, 128), source.reshape(SL * 32, 128), mean_coef.reshape(32, 128),
        var_coefs.reshape(TERMS * 32, 128), jnp.swapaxes(galerkin_cols, 1, 2), jnp.swapaxes(galerkin_vals, 1, 2),
    )
    anywhere = pl.BlockSpec(memory_space=pl.ANY)
    smoothed, coarse = pl.pallas_call(
        store,
        out_shape=(jax.ShapeDtypeStruct((SL * 32, 128), F32), jax.ShapeDtypeStruct((SL * 8, 128), F32)),
        in_specs=[whole] * 2,
        out_specs=(anywhere, anywhere),
        scratch_shapes=[pltpu.SemaphoreType.DMA((2,))],
        name="store",
    )(pltpu.with_memory_space_constraint(smoothed, pltpu.VMEM), pltpu.with_memory_space_constraint(coarse, pltpu.VMEM))
    return smoothed.reshape(field.shape), coarse[:, 0:64].reshape(SL, 2, 4, 64)


def solution(mesh):
    wide = P("chaos", "gx", "gy", None)
    return jax.shard_map(
        body,
        mesh=mesh,
        in_specs=(wide, wide, P("gx", "gy", None), P(None, "gx", "gy", None), P(), P()),
        out_specs=(wide, wide),
        check_vma=False,
    )
```

```python
import jax
import jax.numpy as jnp
from jax import lax
from jax.experimental import pallas as pl
from jax.experimental.pallas import tpu as pltpu
from jax.sharding import PartitionSpec as P


P_SIZE = 66
MESH = pl.DeviceIdType.MESH
SL = 17
OWN = 136
VEC = 72
ALL = 8 * VEC
TERMS = 10
KSEG = 80
F32 = jnp.float32
BF16 = jnp.bfloat16


def lanes(rows):
    return lax.broadcasted_iota(jnp.int32, (rows, 128), 1)


def swing(a):
    return pltpu.roll(a, 64, 1)


def kernel(
    field_in, source_in, mean_in, var_in, cols_in, vals_in, smoothed, coarse,
    field, source, mean, var, cols, vals, loads,
    fs, ss, cs, fr, sr, cr, v1, v2, xlo1, xhi1, ylo1, yhi1, z1, xlo2, xhi2, ylo2, yhi2, z2, zfull,
    ysend1, ysend2, lap, rhs, left, left16, gt, gt2, srcv, after, wz, bs, br, dbuf, cms, cxs, cys, cxys, cmr, cxr, cyr, cxyr,
    send, recv,
):
    gx, gy, ch = lax.axis_index("gx"), lax.axis_index("gy"), lax.axis_index("chaos")
    hi, core = ch // 2, ch % 2
    chip = hi * 4 + gy
    pos = (chip + 6) % 8
    side, blk = pos // 4, pos % 4
    xi = gx * 2 + core
    last_x = 2 * lax.axis_size("gx") - 1

    far_gy = (gy + 2) % 4

    def worker(s, c):
        return (gx, far_gy, (((gy + 2 + 4 * s) % 8) // 4) * 2 + c)

    def owner(j):
        return (gx, far_gy, j)

    def place(dx, dy):
        x, d = xi + dx, (chip + dy + 8) % 8
        return (x // 2, d % 4, (d // 4) * 2 + x % 2)

    has_xp, has_xn = xi > 0, xi < last_x
    has_yp, has_yn = blk > 0, blk < 3
    across = (gx, gy, (1 - hi) * 2 + core)

    barrier = pltpu.get_barrier_semaphore()
    neighbours = [
        (has_xp, place(-1, 0)), (has_xn, place(1, 0)), (has_yp, place(0, -1)), (has_yn, place(0, 1)),
    ]
    more_y, more_x = gy > 0, gx > 0
    for s in range(2):
        lower = ((gy + 1 + 4 * s) % 8) // 4 * 2
        for c in range(2):
            neighbours.append((more_y, (gx, (gy + 1) % 4, lower + c)))
        neighbours.append((more_x, (gx - 1, far_gy, worker(s, 1)[2])))
        neighbours.append((jnp.logical_and(more_x, more_y), (gx - 1, (gy + 1) % 4, lower + 1)))
    for j in range(4):
        pl.semaphore_signal(barrier, inc=1, device_id=owner(j), device_id_type=MESH)
    pl.semaphore_signal(barrier, inc=1, device_id=across, device_id_type=MESH)
    for cond, dev in neighbours:
        @pl.when(cond)
        def _():
            pl.semaphore_signal(barrier, inc=1, device_id=dev, device_id_type=MESH)

    def plane_pair(ref, c):
        return ref.reshape(SL, 32, 128).at[:, pl.ds(16 * c, 16), :]

    pairs = (
        (plane_pair(field_in, 0), plane_pair(field, 0)), (var_in, var), (mean_in, mean), (source_in, source), (cols_in, cols), (vals_in, vals),
        (plane_pair(field_in, 1), plane_pair(field, 1)),
    )
    staged = [pltpu.make_async_copy(a, b, loads.at[i]) for i, (a, b) in enumerate(pairs)]
    for i in (0, 6, 1, 2, 3, 4, 5):
        staged[i].start()

    keep = (lax.broadcasted_iota(jnp.int32, (16, 128), 0) + SL * ch < P_SIZE)
    keep_tail = SL * ch + 16 < P_SIZE
    low16, low8 = lanes(16) < 64, lanes(8) < 64

    def tails(t):
        r = pltpu.roll(swing(t), 4, 0)
        return jnp.where(low8, t, r), swing(jnp.where(low8, r, t))

    def pack(ref, out, planes=range(4)):
        for x in planes:
            c, xl = x // 2, x % 2
            for y in range(4):
                v = xl * 4 + y
                a = jnp.where(keep, ref[pl.ds(x * 8 + y, 16, stride=32), :], 0.0)
                b = swing(jnp.where(keep, ref[pl.ds(x * 8 + y + 4, 16, stride=32), :], 0.0))
                out[pl.ds(c * OWN + v * 16, 16), :] = jnp.where(low16, a, b)
                out[pl.ds((2 + c) * OWN + v * 16, 16), :] = swing(jnp.where(low16, b, a))
            ta, tb = tails(jnp.where(keep_tail, ref[pl.ds(512 + x * 8, 8), :], 0.0))
            out[pl.ds(c * OWN + 128 + xl * 4, 4), :] = ta[0:4]
            out[pl.ds((2 + c) * OWN + 128 + xl * 4, 4), :] = tb[0:4]

    def piece(ref, i):
        return ref.at[pl.ds(pl.multiple_of(i * OWN, 8), OWN), :]

    def copy(src, dst, k, l, dev):
        return pltpu.make_async_remote_copy(
            src_ref=src, dst_ref=dst, send_sem=send.at[k], recv_sem=recv.at[l], device_id=dev, device_id_type=MESH
        )

    staged[0].wait()
    pack(field, fs, (0, 1))
    pl.semaphore_wait(barrier, 5 + sum(jnp.where(cond, 1, 0) for cond, dev in neighbours[0:4])
                      + jnp.where(has_yn, 4, 0) + 4 * core * jnp.where(has_xn, 1, 0) * jnp.where(has_yn, 2, 1))

    for c in range(2):
        if c == 1:
            staged[6].wait()
            pack(field, fs, (2, 3))
        for s in range(2):
            copy(piece(fs, 2 * s + c), piece(fr, ch), 2 * s + c, ch, worker(s, c)).start()

    staged[1].wait()
    staged[2].wait()
    for k in range(TERMS + 1):
        for xl in range(2):
            if k < TERMS:
                t = var[pl.ds(pl.multiple_of(k * 32 + core * 16 + xl * 8, 8), 8), :]
            else:
                t = mean[pl.ds(pl.multiple_of(core * 16 + xl * 8, 8), 8), :]
            ta, tb = tails(t)
            cs[pl.ds(k * 8 + xl * 4, 4), :] = jnp.where(hi == 0, ta, tb)[0:4]
    coefs = copy(cs, cr, 8, 8, worker(hi, core))
    coefs.start()

    staged[3].wait()
    pack(source, ss)

    zero_vec = jnp.zeros((VEC, 128), F32)
    for cond, xref, yref in ((xi == 0, (xlo1, xlo2), ()), (xi == last_x, (xhi1, xhi2), ()),
                             (blk == 0, (), (ylo1, ylo2)), (blk == 3, (), (yhi1, yhi2))):
        @pl.when(cond)
        def _():
            for ref in xref:
                for i in range(4):
                    ref[pl.ds(i * VEC, VEC), :] = zero_vec
            for ref in yref:
                ref[...] = zero_vec

    def clear(ref, n, rows):
        for r in rows:
            ref[pl.ds(r * n, n), :] = jnp.zeros((n, 128), F32)

    @pl.when(gx == 0)
    def _():
        clear(cxr, 32, (0, 2))

    @pl.when(gy == 0)
    def _():
        clear(cyr, 16, range(4))
        clear(cxyr, 16, range(4))

    @pl.when(jnp.logical_and(gx == 0, gy > 0))
    def _():
        clear(cxyr, 16, (0, 2))

    clear(cms, 32, range(4))
    clear(cxs, 32, range(4))
    clear(cys, 16, range(4))
    clear(cxys, 16, range(4))

    lane72 = lanes(VEC)
    low = lane72 < 64
    z64 = jnp.bitwise_and(lane72, 63)
    edge = 63 * (1 - side)
    edge_lane = z64 == edge
    first_lane, end_lane = z64 == 0, z64 == 63

    def vec(ref, v):
        return ref[pl.ds(v * VEC, VEC), :]

    def gather(src, dst):
        for v in range(8):
            for j in range(4):
                dst[pl.ds(v * VEC + 16 * j, 16), :] = src[pl.ds(j * OWN + 16 * v, 16), :]
            dst[pl.ds(v * VEC + 64, 4), :] = src[pl.ds(128 + v, 4, stride=OWN), :]
            dst[pl.ds(v * VEC + 68, 4), :] = jnp.zeros((4, 128), F32)

    def arrived(dst, k, l):
        copy(dst, dst, k, l, across).wait_recv()

    def spread(val, stage, halos, base):
        xlo, xhi, ylo, yhi, z, zfull = halos
        up = stage.at[pl.ds(0, VEC), :]
        down = stage.at[pl.ds(VEC, VEC), :]
        zs = stage.at[pl.ds(2 * VEC, 16), :]
        xn = copy(val.at[pl.ds(4 * VEC, 4 * VEC), :], xlo, base, base, place(1, 0))
        xp = copy(val.at[pl.ds(0, 4 * VEC), :], xhi, base + 1, base + 1, place(-1, 0))
        yn = copy(up, ylo, base + 2, base + 2, place(0, 1))
        yp = copy(down, yhi, base + 3, base + 3, place(0, -1))
        zc = copy(zs, z, base + 4, base + 4, across)

        @pl.when(has_xn)
        def _():
            xn.start()

        @pl.when(has_xp)
        def _():
            xp.start()

        total = zero_vec
        for v in range(8):
            total = jnp.where(z64 == v, pltpu.roll(vec(val, v), v + 65 * (1 - side), 1), total)
        for t in range(8):
            part = total[8 * t:8 * t + 8]
            packed = jnp.where(z64[0:8] // 8 == t, pltpu.roll(part, 8 * t, 1) if t else part, packed) if t else part
        stage[pl.ds(2 * VEC, 8), :] = packed
        stage[pl.ds(2 * VEC + 8, 8), :] = total[64:72]
        zc.start()

        up[...] = jnp.where(low, swing(vec(val, 3)), vec(val, 7))
        down[...] = jnp.where(low, vec(val, 0), swing(vec(val, 4)))

        @pl.when(has_yn)
        def _():
            yn.start()

        @pl.when(has_yp)
        def _():
            yp.start()

        return xn, xp, yn, yp, zc

    def collect_x(ops):
        xn, xp, yn, yp, zc = ops

        @pl.when(has_xp)
        def _():
            xn.wait_recv()

        @pl.when(has_xn)
        def _():
            xp.wait_recv()

    def collect(ops):
        xn, xp, yn, yp, zc = ops

        @pl.when(has_yp)
        def _():
            yn.wait_recv()

        @pl.when(has_yn)
        def _():
            yp.wait_recv()

        zc.wait_recv()

    def laplace(val, halos, ops):
        xlo, xhi, ylo, yhi, zpacked, z = halos
        for t in range(8):
            z[pl.ds(8 * t, 8), :] = pltpu.roll(zpacked[0:8, :], (128 - 8 * t) % 128, 1) if t else zpacked[0:8, :]
        z[pl.ds(64, 8), :] = zpacked[8:16, :]
        for x in range(2):
            for y in range(4):
                v = 4 * x + y
                here = vec(val, v)
                beside = vec(val, v - 4) if x else vec(val, v + 4)
                if y > 0:
                    beside = beside + vec(val, v - 1)
                elif x == 0:
                    beside = beside + jnp.where(low, ylo[...], swing(vec(val, 3)))
                else:
                    beside = beside + swing(jnp.where(low, vec(val, 7), ylo[...]))
                if y < 3:
                    beside = beside + vec(val, v + 1)
                elif x == 0:
                    beside = beside + swing(jnp.where(low, yhi[...], vec(val, 0)))
                else:
                    beside = beside + jnp.where(low, swing(vec(val, 4)), yhi[...])
                beside = beside + jnp.where(first_lane, 0.0, pltpu.roll(here, 1, 1))
                beside = beside + jnp.where(end_lane, 0.0, pltpu.roll(here, 127, 1))
                beside = beside + jnp.where(edge_lane, pltpu.roll(z[...], (edge + 128 - v) % 128, 1), 0.0)
                out = 6.0 * here - beside
                lap[pl.ds(v * VEC, VEC), :] = out
        collect_x(ops)
        for x in range(2):
            for y in range(4):
                v = 4 * x + y
                out = vec(lap, v) - vec(xhi if x else xlo, y)
                lap[pl.ds(v * VEC, VEC), :] = out
                b1 = out.astype(BF16)
                b2 = (out - b1.astype(F32)).astype(BF16)
                r, h = (v // 2) * 256, (v % 2) * 128
                rhs[r:r + VEC, h:h + 128] = b1
                rhs[r + KSEG:r + KSEG + VEC, h:h + 128] = b2
                rhs[r + 2 * KSEG:r + 2 * KSEG + VEC, h:h + 128] = b1

    def operate(use):
        def step(q, carry):
            mixed = jnp.dot(
                left16[...], rhs[pl.ds(pl.multiple_of(q * 256, 256), 256), :], preferred_element_type=F32
            )
            for h in range(2):
                v = 2 * q + h
                rows = pl.ds(pl.multiple_of(v * VEC, 8), VEC)
                m = cr[pl.ds(TERMS * 8 + v, 1), :]
                total = m * lap[rows, :]
                for k in range(TERMS):
                    total = total + cr[pl.ds(k * 8 + v, 1), :] * mixed[k * VEC:(k + 1) * VEC, h * 128:(h + 1) * 128]
                use(rows, m, total)
            return carry

        lax.fori_loop(0, 4, step, 0, unroll=4)

    for j in range(4):
        arrived(piece(fr, j), j, j)
    gather(fr, v1)
    halos1 = (xlo1, xhi1, ylo1, yhi1, z1, zfull)
    ops1 = spread(v1, ysend1, halos1, 9)
    for c in range(2):
        for s in range(2):
            copy(piece(ss, 2 * s + c), piece(sr, ch), 4 + 2 * s + c, 4 + ch, worker(s, c)).start()
    rhs[...] = jnp.zeros((4 * 256, 256), BF16)
    gt[...] = jnp.zeros((128, 128), F32)
    staged[4].wait()
    staged[5].wait()
    p = lax.broadcasted_iota(jnp.int32, (KSEG, 68), 0)
    slot = jnp.where(p < 64, SL * lax.shift_right_logical(p, 4) + jnp.bitwise_and(p, 15),
                     jnp.where(p < 68, SL * (p - 64) + 16, -1))
    used = lax.broadcasted_iota(jnp.int32, (1, 68), 1) < P_SIZE

    def build(k, carry):
        total = jnp.zeros((KSEG, 68), F32)
        for b in range(3):
            total = total + jnp.where(slot == cols[k, b:b + 1, :], jnp.where(used, vals[k, b:b + 1, :], 0.0), 0.0)
        gt[0:KSEG, 0:68] = total
        gt2[...] = jnp.transpose(gt[...])
        rows = [gt2[pl.ds(SL * j, 16), :] for j in range(4)]
        rows.append(gt2[pl.ds(16, 4, stride=SL), :])
        rows.append(jnp.zeros((4, 128), F32))
        g = jnp.concatenate(rows, 0)
        a1 = g.astype(BF16).astype(F32)
        a2 = g - a1
        r = pltpu.roll(a1, KSEG, 1)
        left[pl.ds(pl.multiple_of(k * VEC, 8), VEC), 0:128] = jnp.where(lane72 < 80, a1, r)
        left[pl.ds(pl.multiple_of(k * VEC, 8), VEC), 128:256] = jnp.where(lane72 < 32, r, pltpu.roll(a2, 32, 1))
        return carry

    lax.fori_loop(0, TERMS, build, 0)
    left16[...] = left[...].astype(BF16)

    arrived(cr, 8, 8)
    collect(ops1)
    laplace(v1, halos1, ops1)

    def keep_total(rows, m, total):
        after[rows, :] = total

    operate(keep_total)
    for j in range(4):
        arrived(piece(sr, j), 4 + j, 4 + j)
    gather(sr, srcv)
    for v in range(8):
        first = vec(srcv, v) - vec(after, v)
        v2[pl.ds(v * VEC, VEC), :] = vec(v1, v) + (2.0 / 3.0) * first / (6.0 * cr[pl.ds(TERMS * 8 + v, 1), :])

    halos2 = (xlo2, xhi2, ylo2, yhi2, z2, zfull)
    ops2 = spread(v2, ysend2, halos2, 14)
    for j in range(4):
        for v in range(8):
            bs[pl.ds(j * OWN + 16 * v, 16), :] = v2[pl.ds(v * VEC + 16 * j, 16), :]
        bs[pl.ds(j * OWN + 128, 8), :] = v2[pl.ds(64 + j, 8, stride=VEC), :]
    here = 2 * side + core
    for j in range(4):
        copy(piece(bs, j), piece(br, here), 19 + j, 19 + here, owner(j)).start()
    row = lax.broadcasted_iota(jnp.int32, (256, 256), 0)
    col = lax.broadcasted_iota(jnp.int32, (256, 256), 1)
    half = jnp.bitwise_and(lax.shift_right_logical(row, 6), 1)
    b_row = 2 * half + lax.shift_right_logical(row, 7)
    z_row = jnp.bitwise_and(row, 63)
    off = z_row - 2 * jnp.bitwise_and(col, 31)
    near = jnp.where(off == 0, 0.5, jnp.where(jnp.logical_or(off == 1, off == -1), 0.25, 0.0))
    main_w = jnp.where(jnp.logical_and(col < 128, lax.shift_right_logical(col, 5) == b_row), near, 0.0)
    next_w = jnp.where(jnp.logical_and(col == 128 + b_row, z_row == 63), 0.25, 0.0)
    wz[...] = (main_w + next_w).astype(BF16)

    collect(ops2)
    laplace(v2, halos2, ops2)

    def residual(rows, m, total):
        after[rows, :] = srcv[rows, :] - total

    operate(residual)

    for i in range(2):
        if i == 0:
            c = [0.5 * vec(after, y) + 0.25 * vec(after, 4 + y) for y in range(4)]
        else:
            c = [0.25 * vec(after, 4 + y) for y in range(4)]
        s3 = 0.25 * swing(c[3])
        d0 = 0.5 * c[0] + 0.25 * c[1] + jnp.where(low, 0.0, s3)
        d1 = 0.5 * c[2] + 0.25 * (c[3] + c[1])
        dn = jnp.where(low, s3, 0.0)
        for r, (da, db) in ((i, (d0, d1)), (2 + i, (dn, None))):
            for h, d in ((0, da), (1, db)):
                if d is None:
                    d = zero_vec
                dh = d.astype(BF16)
                dbuf[pl.ds(r * VEC, VEC), h * 128:(h + 1) * 128] = dh.astype(F32)
                dbuf[pl.ds((4 + r) * VEC, VEC), h * 128:(h + 1) * 128] = d - dh.astype(F32)
    parts = jnp.dot(dbuf[...].astype(BF16), wz[...], preferred_element_type=F32)
    parts = parts[0:4 * VEC] + parts[4 * VEC:8 * VEC]

    def both(r):
        return parts[r * VEC:(r + 1) * VEC, 0:128], parts[r * VEC:(r + 1) * VEC, 128:256]

    lane8 = lanes(8)

    def wide(out, r):
        a, b = both(r)
        for j in range(4):
            out[pl.ds(j * 32, 16), :] = a[16 * j:16 * j + 16]
            out[pl.ds(j * 32 + 16, 8), :] = jnp.where(
                lane8 < 8, b[16 * j:16 * j + 8], pltpu.roll(b[16 * j + 8:16 * j + 16], 8, 1)
            )
            out[pl.ds(j * 32 + 24, 1), :] = a[64 + j:65 + j]
            out[pl.ds(j * 32 + 25, 1), :] = b[64 + j:65 + j]

    def slim(out, r):
        a, b = both(r)
        w = a + pltpu.roll(b, 32, 1)
        for j in range(4):
            out[pl.ds(j * 16, 8), :] = w[16 * j:16 * j + 8] + pltpu.roll(w[16 * j + 8:16 * j + 16], 64, 1)
            out[pl.ds(j * 16 + 8, 1), :] = w[64 + j:65 + j]

    def cut(ref, i, n):
        return ref.at[pl.ds(pl.multiple_of(i * n, 8), n), :]

    def parted(src, dst, n, base, slot, dx, dy):
        return [
            copy(cut(src, j, n), cut(dst, slot, n), base + j, base + slot, (gx + dx, far_gy + dy, j)) for j in range(4)
        ]

    there = 2 * side + 1 - core
    has_xyn = jnp.logical_and(has_xn, has_yn)
    results = []
    for fill, r, src, dst, n, base, slot, dx, dy, cond in (
        (wide, 1, cxs, cxr, 32, 30, there, core, 0, has_xn), (slim, 3, cxys, cxyr, 16, 38, there, core, 1, has_xyn),
        (slim, 2, cys, cyr, 16, 34, here, 0, 1, has_yn), (wide, 0, cms, cmr, 32, 26, here, 0, 0, gx >= 0),
    ):
        fill(src, r)
        ops = parted(src, dst, n, base, slot, dx, dy)
        results.append((cond, ops))

        @pl.when(cond)
        def _():
            for op in ops:
                op.start()

    for j in range(4):
        arrived(piece(br, j), 19 + j, 19 + j)
    for x in range(4):
        c, xl = x // 2, x % 2
        for y in range(4):
            v = 4 * xl + y
            va = br[pl.ds(c * OWN + 16 * v, 16), :]
            vb = br[pl.ds((2 + c) * OWN + 16 * v, 16), :]
            smoothed[pl.ds(x * 8 + y, 16, stride=32), :] = jnp.where(low16, va, swing(vb))
            smoothed[pl.ds(x * 8 + y + 4, 16, stride=32), :] = jnp.where(low16, swing(va), vb)
        ta = br[pl.ds(c * OWN + 128, 8), :]
        tb = br[pl.ds((2 + c) * OWN + 128, 8), :]
        smoothed[pl.ds(512 + x * 8, 4), :] = jnp.where(low8, ta, swing(tb))[4 * xl:4 * xl + 4]
        smoothed[pl.ds(512 + x * 8 + 4, 4), :] = jnp.where(low8, swing(ta), tb)[4 * xl:4 * xl + 4]

    for i in range(4):
        arrived(cut(cmr, i, 32), 26, 26 + i)

        @pl.when(more_x if i % 2 == 0 else gx >= 0)
        def _():
            arrived(cut(cxr, i, 32), 30, 30 + i)

        @pl.when(more_y)
        def _():
            arrived(cut(cyr, i, 16), 34, 34 + i)

        @pl.when(jnp.logical_and(more_x, more_y) if i % 2 == 0 else more_y)
        def _():
            arrived(cut(cxyr, i, 16), 38, 38 + i)

    lane16 = lanes(16)

    def unite(i):
        m = cmr[pl.ds(i * 32, 16), :] + cxr[pl.ds(i * 32, 16), :]
        zp = cmr[pl.ds(i * 32 + 16, 8), :] + cxr[pl.ds(i * 32 + 16, 8), :]
        t = cmr[pl.ds(i * 32 + 24, 8), :] + cxr[pl.ds(i * 32 + 24, 8), :]
        yp = cyr[pl.ds(i * 16, 8), :] + cxyr[pl.ds(i * 16, 8), :]
        yt = cyr[pl.ds(i * 16 + 8, 8), :] + cxyr[pl.ds(i * 16 + 8, 8), :]
        z = jnp.concatenate([zp, pltpu.roll(zp, 120, 1)], 0)
        y = jnp.concatenate([yp, swing(yp)], 0)
        m = m + jnp.where(lane16 < 32, y, 0.0)
        return m, z, y, t + jnp.where(lane8 < 32, yt, 0.0), pltpu.roll(t, 7, 0), yt

    for x in range(2):
        ma, za, ya, ta, zt, yt = unite(x)
        mb, _, _, tb, _, _ = unite(2 + x)
        for b in range(4):
            def joined(left_, right_, extra, edge_y, lane):
                out = jnp.where(lane < 32, pltpu.roll(left_, (128 - 32 * b) % 128, 1), pltpu.roll(right_, (160 - 32 * b) % 128, 1))
                extra = pltpu.roll(extra, 32 - b, 1)
                return out + jnp.where(lane == 32, extra + edge_y if b == 0 else extra, 0.0)

            coarse[pl.ds(x * 4 + b, 16, stride=8), :] = joined(ma, mb, za, ya, lane16)
            coarse[pl.ds(128 + x * 4 + b, 1), :] = joined(ta, tb, zt, yt, lane8)[0:1]

    for j in range(4):
        copy(piece(fs, j), piece(fr, j), j, j, across).wait_send()
        copy(piece(ss, j), piece(sr, j), 4 + j, 4 + j, across).wait_send()
        copy(piece(bs, j), piece(br, j), 19 + j, 19 + j, across).wait_send()
    coefs.wait_send()
    for xn, xp, yn, yp, zc in (ops1, ops2):
        zc.wait_send()
        for cond, op in ((has_xn, xn), (has_xp, xp), (has_yn, yn), (has_yp, yp)):
            @pl.when(cond)
            def _():
                op.wait_send()
    for cond, ops in results:
        @pl.when(cond)
        def _():
            for op in ops:
                op.wait_send()


def scratch():
    def rows(n, width=128, kind=F32):
        return pltpu.VMEM((n, width), kind)

    halos = [rows(4 * VEC), rows(4 * VEC), rows(VEC), rows(VEC), rows(16)]
    return [
        rows(SL * 32), rows(SL * 32), rows(32), rows(TERMS * 32), pltpu.VMEM((TERMS, 3, 4 * SL), jnp.int32),
        pltpu.VMEM((TERMS, 3, 4 * SL), F32), pltpu.SemaphoreType.DMA((7,)),
        rows(4 * OWN), rows(4 * OWN), rows(8 * (TERMS + 1)), rows(4 * OWN), rows(4 * OWN), rows(8 * (TERMS + 1)),
        rows(ALL), rows(ALL), *halos, *halos, rows(VEC), rows(2 * VEC + 16), rows(2 * VEC + 16), rows(ALL), rows(4 * 256, 256, BF16),
        rows(TERMS * VEC, 256), rows(TERMS * VEC, 256, BF16), rows(128), rows(128), rows(ALL), rows(ALL), rows(256, 256, BF16),
        rows(4 * OWN), rows(4 * OWN), rows(8 * VEC, 256), rows(128), rows(128), rows(64), rows(64),
        rows(128), rows(128), rows(64), rows(64),
        pltpu.SemaphoreType.DMA((42,)), pltpu.SemaphoreType.DMA((42,)),
    ]


def store(smoothed, coarse, smoothed_out, coarse_out, sems):
    ops = [
        pltpu.make_async_copy(smoothed, smoothed_out, sems.at[0]), pltpu.make_async_copy(coarse, coarse_out, sems.at[1]),
    ]
    for op in ops:
        op.start()
    for op in ops:
        op.wait()


def body(field, source, mean_coef, var_coefs, galerkin_cols, galerkin_vals):
    whole = pl.BlockSpec(memory_space=pltpu.VMEM)
    smoothed, coarse = pl.pallas_call(
        kernel,
        out_shape=(pltpu.VMEM((SL * 32, 128), F32), pltpu.VMEM((SL * 8, 128), F32)),
        in_specs=[pl.BlockSpec(memory_space=pl.ANY)] * 6,
        out_specs=(whole, whole),
        scratch_shapes=scratch(),
        compiler_params=pltpu.CompilerParams(collective_id=0, has_side_effects=True),
        name="sweep",
    )(
        field.reshape(SL * 32, 128), source.reshape(SL * 32, 128), mean_coef.reshape(32, 128),
        var_coefs.reshape(TERMS * 32, 128), jnp.swapaxes(galerkin_cols, 1, 2), jnp.swapaxes(galerkin_vals, 1, 2),
    )
    anywhere = pl.BlockSpec(memory_space=pl.ANY)
    smoothed, coarse = pl.pallas_call(
        store,
        out_shape=(jax.ShapeDtypeStruct((SL * 32, 128), F32), jax.ShapeDtypeStruct((SL * 8, 128), F32)),
        in_specs=[whole] * 2,
        out_specs=(anywhere, anywhere),
        scratch_shapes=[pltpu.SemaphoreType.DMA((2,))],
        name="store",
    )(pltpu.with_memory_space_constraint(smoothed, pltpu.VMEM), pltpu.with_memory_space_constraint(coarse, pltpu.VMEM))
    return smoothed.reshape(field.shape), coarse[:, 0:64].reshape(SL, 2, 4, 64)


def solution(mesh):
    wide = P("chaos", "gx", "gy", None)
    return jax.shard_map(
        body,
        mesh=mesh,
        in_specs=(wide, wide, P("gx", "gy", None), P(None, "gx", "gy", None), P(), P()),
        out_specs=(wide, wide),
        check_vma=False,
    )
```

```python
import jax
import jax.numpy as jnp
from jax import lax
from jax.experimental import pallas as pl
from jax.experimental.pallas import tpu as pltpu
from jax.sharding import PartitionSpec as P


P_SIZE = 66
MESH = pl.DeviceIdType.MESH
SL = 17
OWN = 136
VEC = 72
ALL = 8 * VEC
TERMS = 10
KSEG = 80
F32 = jnp.float32
BF16 = jnp.bfloat16


def lanes(rows):
    return lax.broadcasted_iota(jnp.int32, (rows, 128), 1)


def swing(a):
    return pltpu.roll(a, 64, 1)


def kernel(
    field_in, source_in, mean_in, var_in, cols_in, vals_in, smoothed, coarse,
    field, source, mean, var, cols, vals, loads,
    fs, ss, cs, fr, sr, cr, v1, v2, xlo1, xhi1, ylo1, yhi1, z1, xlo2, xhi2, ylo2, yhi2, z2, zfull,
    ysend1, ysend2, lap, rhs, left, left16, gt, gt2, srcv, after, wz, bs, br, dbuf, factor, cms, cxs, cys, cxys, cmr, cxr, cyr, cxyr,
    send, recv,
):
    gx, gy, ch = lax.axis_index("gx"), lax.axis_index("gy"), lax.axis_index("chaos")
    hi, core = ch // 2, ch % 2
    chip = hi * 4 + gy
    pos = (chip + 6) % 8
    side, blk = pos // 4, pos % 4
    xi = gx * 2 + core
    last_x = 2 * lax.axis_size("gx") - 1

    far_gy = (gy + 2) % 4

    def worker(s, c):
        return (gx, far_gy, (((gy + 2 + 4 * s) % 8) // 4) * 2 + c)

    def owner(j):
        return (gx, far_gy, j)

    def place(dx, dy):
        x, d = xi + dx, (chip + dy + 8) % 8
        return (x // 2, d % 4, (d // 4) * 2 + x % 2)

    has_xp, has_xn = xi > 0, xi < last_x
    has_yp, has_yn = blk > 0, blk < 3
    across = (gx, gy, (1 - hi) * 2 + core)

    barrier = pltpu.get_barrier_semaphore()
    neighbours = [
        (has_xp, place(-1, 0)), (has_xn, place(1, 0)), (has_yp, place(0, -1)), (has_yn, place(0, 1)),
    ]
    more_y, more_x = gy > 0, gx > 0
    for s in range(2):
        lower = ((gy + 1 + 4 * s) % 8) // 4 * 2
        for c in range(2):
            neighbours.append((more_y, (gx, (gy + 1) % 4, lower + c)))
        neighbours.append((more_x, (gx - 1, far_gy, worker(s, 1)[2])))
        neighbours.append((jnp.logical_and(more_x, more_y), (gx - 1, (gy + 1) % 4, lower + 1)))
    for j in range(4):
        pl.semaphore_signal(barrier, inc=1, device_id=owner(j), device_id_type=MESH)
    pl.semaphore_signal(barrier, inc=1, device_id=across, device_id_type=MESH)
    for cond, dev in neighbours:
        @pl.when(cond)
        def _():
            pl.semaphore_signal(barrier, inc=1, device_id=dev, device_id_type=MESH)

    def plane_pair(ref, c):
        return ref.reshape(SL, 32, 128).at[:, pl.ds(16 * c, 16), :]

    pairs = (
        (plane_pair(field_in, 0), plane_pair(field, 0)), (var_in, var), (mean_in, mean), (source_in, source), (cols_in, cols), (vals_in, vals),
        (plane_pair(field_in, 1), plane_pair(field, 1)),
    )
    staged = [pltpu.make_async_copy(a, b, loads.at[i]) for i, (a, b) in enumerate(pairs)]
    for i in (0, 6, 1, 2, 3, 4, 5):
        staged[i].start()

    keep = (lax.broadcasted_iota(jnp.int32, (16, 128), 0) + SL * ch < P_SIZE)
    keep_tail = SL * ch + 16 < P_SIZE
    low16, low8 = lanes(16) < 64, lanes(8) < 64

    def tails(t):
        r = pltpu.roll(swing(t), 4, 0)
        return jnp.where(low8, t, r), swing(jnp.where(low8, r, t))

    def pack(ref, out, planes=range(4)):
        for x in planes:
            c, xl = x // 2, x % 2
            for y in range(4):
                v = xl * 4 + y
                a = jnp.where(keep, ref[pl.ds(x * 8 + y, 16, stride=32), :], 0.0)
                b = swing(jnp.where(keep, ref[pl.ds(x * 8 + y + 4, 16, stride=32), :], 0.0))
                out[pl.ds(c * OWN + v * 16, 16), :] = jnp.where(low16, a, b)
                out[pl.ds((2 + c) * OWN + v * 16, 16), :] = swing(jnp.where(low16, b, a))
            ta, tb = tails(jnp.where(keep_tail, ref[pl.ds(512 + x * 8, 8), :], 0.0))
            out[pl.ds(c * OWN + 128 + xl * 4, 4), :] = ta[0:4]
            out[pl.ds((2 + c) * OWN + 128 + xl * 4, 4), :] = tb[0:4]

    def piece(ref, i):
        return ref.at[pl.ds(pl.multiple_of(i * OWN, 8), OWN), :]

    def copy(src, dst, k, l, dev):
        return pltpu.make_async_remote_copy(
            src_ref=src, dst_ref=dst, send_sem=send.at[k], recv_sem=recv.at[l], device_id=dev, device_id_type=MESH
        )

    staged[0].wait()
    pack(field, fs, (0, 1))
    pl.semaphore_wait(barrier, 5 + sum(jnp.where(cond, 1, 0) for cond, dev in neighbours[0:4])
                      + jnp.where(has_yn, 4, 0) + 4 * core * jnp.where(has_xn, 1, 0) * jnp.where(has_yn, 2, 1))

    for c in range(2):
        if c == 1:
            staged[6].wait()
            pack(field, fs, (2, 3))
        for s in range(2):
            copy(piece(fs, 2 * s + c), piece(fr, ch), 2 * s + c, ch, worker(s, c)).start()

    staged[1].wait()
    staged[2].wait()
    for k in range(TERMS + 1):
        for xl in range(2):
            if k < TERMS:
                t = var[pl.ds(pl.multiple_of(k * 32 + core * 16 + xl * 8, 8), 8), :]
            else:
                t = mean[pl.ds(pl.multiple_of(core * 16 + xl * 8, 8), 8), :]
            ta, tb = tails(t)
            cs[pl.ds(k * 8 + xl * 4, 4), :] = jnp.where(hi == 0, ta, tb)[0:4]
    coefs = copy(cs, cr, 8, 8, worker(hi, core))
    coefs.start()

    staged[3].wait()
    pack(source, ss)

    zero_vec = jnp.zeros((VEC, 128), F32)
    for cond, xref, yref in ((xi == 0, (xlo1, xlo2), ()), (xi == last_x, (xhi1, xhi2), ()),
                             (blk == 0, (), (ylo1, ylo2)), (blk == 3, (), (yhi1, yhi2))):
        @pl.when(cond)
        def _():
            for ref in xref:
                for i in range(4):
                    ref[pl.ds(i * VEC, VEC), :] = zero_vec
            for ref in yref:
                ref[...] = zero_vec

    def clear(ref, n, rows):
        for r in rows:
            ref[pl.ds(r * n, n), :] = jnp.zeros((n, 128), F32)

    @pl.when(gx == 0)
    def _():
        clear(cxr, 32, (0, 2))

    @pl.when(gy == 0)
    def _():
        clear(cyr, 16, range(4))
        clear(cxyr, 16, range(4))

    @pl.when(jnp.logical_and(gx == 0, gy > 0))
    def _():
        clear(cxyr, 16, (0, 2))

    clear(cms, 32, range(4))
    clear(cxs, 32, range(4))
    clear(cys, 16, range(4))
    clear(cxys, 16, range(4))

    lane72 = lanes(VEC)
    low = lane72 < 64
    z64 = jnp.bitwise_and(lane72, 63)
    edge = 63 * (1 - side)
    edge_lane = z64 == edge
    first_lane, end_lane = z64 == 0, z64 == 63

    def vec(ref, v):
        return ref[pl.ds(v * VEC, VEC), :]

    def gather(src, dst):
        for v in range(8):
            for j in range(4):
                dst[pl.ds(v * VEC + 16 * j, 16), :] = src[pl.ds(j * OWN + 16 * v, 16), :]
            dst[pl.ds(v * VEC + 64, 4), :] = src[pl.ds(128 + v, 4, stride=OWN), :]
            dst[pl.ds(v * VEC + 68, 4), :] = jnp.zeros((4, 128), F32)

    def arrived(dst, k, l):
        copy(dst, dst, k, l, across).wait_recv()

    def spread(val, stage, halos, base):
        xlo, xhi, ylo, yhi, z, zfull = halos
        up = stage.at[pl.ds(0, VEC), :]
        down = stage.at[pl.ds(VEC, VEC), :]
        zs = stage.at[pl.ds(2 * VEC, 16), :]
        xn = copy(val.at[pl.ds(4 * VEC, 4 * VEC), :], xlo, base, base, place(1, 0))
        xp = copy(val.at[pl.ds(0, 4 * VEC), :], xhi, base + 1, base + 1, place(-1, 0))
        yn = copy(up, ylo, base + 2, base + 2, place(0, 1))
        yp = copy(down, yhi, base + 3, base + 3, place(0, -1))
        zc = copy(zs, z, base + 4, base + 4, across)

        @pl.when(has_xn)
        def _():
            xn.start()

        @pl.when(has_xp)
        def _():
            xp.start()

        total = zero_vec
        for v in range(8):
            total = jnp.where(z64 == v, pltpu.roll(vec(val, v), v + 65 * (1 - side), 1), total)
        for t in range(8):
            part = total[8 * t:8 * t + 8]
            packed = jnp.where(z64[0:8] // 8 == t, pltpu.roll(part, 8 * t, 1) if t else part, packed) if t else part
        stage[pl.ds(2 * VEC, 8), :] = packed
        stage[pl.ds(2 * VEC + 8, 8), :] = total[64:72]
        zc.start()

        up[...] = jnp.where(low, swing(vec(val, 3)), vec(val, 7))
        down[...] = jnp.where(low, vec(val, 0), swing(vec(val, 4)))

        @pl.when(has_yn)
        def _():
            yn.start()

        @pl.when(has_yp)
        def _():
            yp.start()

        return xn, xp, yn, yp, zc

    def collect_x(ops):
        xn, xp, yn, yp, zc = ops

        @pl.when(has_xp)
        def _():
            xn.wait_recv()

        @pl.when(has_xn)
        def _():
            xp.wait_recv()

    def collect(ops):
        xn, xp, yn, yp, zc = ops

        @pl.when(has_yp)
        def _():
            yn.wait_recv()

        @pl.when(has_yn)
        def _():
            yp.wait_recv()

        zc.wait_recv()

    def laplace(val, halos, ops):
        xlo, xhi, ylo, yhi, zpacked, z = halos
        for t in range(8):
            z[pl.ds(8 * t, 8), :] = pltpu.roll(zpacked[0:8, :], (128 - 8 * t) % 128, 1) if t else zpacked[0:8, :]
        z[pl.ds(64, 8), :] = zpacked[8:16, :]
        for x in range(2):
            for y in range(4):
                v = 4 * x + y
                here = vec(val, v)
                beside = vec(val, v - 4) if x else vec(val, v + 4)
                if y > 0:
                    beside = beside + vec(val, v - 1)
                elif x == 0:
                    beside = beside + jnp.where(low, ylo[...], swing(vec(val, 3)))
                else:
                    beside = beside + swing(jnp.where(low, vec(val, 7), ylo[...]))
                if y < 3:
                    beside = beside + vec(val, v + 1)
                elif x == 0:
                    beside = beside + swing(jnp.where(low, yhi[...], vec(val, 0)))
                else:
                    beside = beside + jnp.where(low, swing(vec(val, 4)), yhi[...])
                beside = beside + jnp.where(first_lane, 0.0, pltpu.roll(here, 1, 1))
                beside = beside + jnp.where(end_lane, 0.0, pltpu.roll(here, 127, 1))
                beside = beside + jnp.where(edge_lane, pltpu.roll(z[...], (edge + 128 - v) % 128, 1), 0.0)
                out = 6.0 * here - beside
                lap[pl.ds(v * VEC, VEC), :] = out
        collect_x(ops)
        for x in range(2):
            for y in range(4):
                v = 4 * x + y
                out = vec(lap, v) - vec(xhi if x else xlo, y)
                lap[pl.ds(v * VEC, VEC), :] = out
                b1 = out.astype(BF16)
                b2 = (out - b1.astype(F32)).astype(BF16)
                r, h = (v // 2) * 256, (v % 2) * 128
                rhs[r:r + VEC, h:h + 128] = b1
                rhs[r + KSEG:r + KSEG + VEC, h:h + 128] = b2
                rhs[r + 2 * KSEG:r + 2 * KSEG + VEC, h:h + 128] = b1

    def operate(use):
        def step(q, carry):
            mixed = jnp.dot(
                left16[...], rhs[pl.ds(pl.multiple_of(q * 256, 256), 256), :], preferred_element_type=F32
            )
            for h in range(2):
                v = 2 * q + h
                rows = pl.ds(pl.multiple_of(v * VEC, 8), VEC)
                m = cr[pl.ds(TERMS * 8 + v, 1), :]
                total = m * lap[rows, :]
                for k in range(TERMS):
                    total = total + cr[pl.ds(k * 8 + v, 1), :] * mixed[k * VEC:(k + 1) * VEC, h * 128:(h + 1) * 128]
                use(rows, m, total)
            return carry

        lax.fori_loop(0, 4, step, 0, unroll=2)

    for j in range(4):
        arrived(piece(fr, j), j, j)
    gather(fr, v1)
    halos1 = (xlo1, xhi1, ylo1, yhi1, z1, zfull)
    ops1 = spread(v1, ysend1, halos1, 9)
    for c in range(2):
        for s in range(2):
            copy(piece(ss, 2 * s + c), piece(sr, ch), 4 + 2 * s + c, 4 + ch, worker(s, c)).start()
    rhs[...] = jnp.zeros((4 * 256, 256), BF16)
    gt[...] = jnp.zeros((128, 128), F32)
    staged[4].wait()
    staged[5].wait()
    p = lax.broadcasted_iota(jnp.int32, (KSEG, 68), 0)
    slot = jnp.where(p < 64, SL * lax.shift_right_logical(p, 4) + jnp.bitwise_and(p, 15),
                     jnp.where(p < 68, SL * (p - 64) + 16, -1))
    used = lax.broadcasted_iota(jnp.int32, (1, 68), 1) < P_SIZE

    def build(k, carry):
        total = jnp.zeros((KSEG, 68), F32)
        for b in range(3):
            total = total + jnp.where(slot == cols[k, b:b + 1, :], jnp.where(used, vals[k, b:b + 1, :], 0.0), 0.0)
        gt[0:KSEG, 0:68] = total
        gt2[...] = jnp.transpose(gt[...])
        rows = [gt2[pl.ds(SL * j, 16), :] for j in range(4)]
        rows.append(gt2[pl.ds(16, 4, stride=SL), :])
        rows.append(jnp.zeros((4, 128), F32))
        g = jnp.concatenate(rows, 0)
        a1 = g.astype(BF16).astype(F32)
        a2 = g - a1
        r = pltpu.roll(a1, KSEG, 1)
        left[pl.ds(pl.multiple_of(k * VEC, 8), VEC), 0:128] = jnp.where(lane72 < 80, a1, r)
        left[pl.ds(pl.multiple_of(k * VEC, 8), VEC), 128:256] = jnp.where(lane72 < 32, r, pltpu.roll(a2, 32, 1))
        return carry

    lax.fori_loop(0, TERMS, build, 0)
    left16[...] = left[...].astype(BF16)

    arrived(cr, 8, 8)
    collect(ops1)
    laplace(v1, halos1, ops1)

    def keep_total(rows, m, total):
        after[rows, :] = total

    operate(keep_total)
    factor[...] = (2.0 / 3.0) / (6.0 * cr[pl.ds(TERMS * 8, 8), :])
    for j in range(4):
        arrived(piece(sr, j), 4 + j, 4 + j)
        for v in range(8):
            rows = pl.ds(v * VEC + 16 * j, 16)
            v2[rows, :] = v1[rows, :] + factor[pl.ds(v, 1), :] * (sr[pl.ds(j * OWN + 16 * v, 16), :] - after[rows, :])
    for v in range(8):
        rows = pl.ds(v * VEC + 64, 4)
        v2[rows, :] = v1[rows, :] + factor[pl.ds(v, 1), :] * (sr[pl.ds(128 + v, 4, stride=OWN), :] - after[rows, :])
        v2[pl.ds(v * VEC + 68, 4), :] = jnp.zeros((4, 128), F32)

    halos2 = (xlo2, xhi2, ylo2, yhi2, z2, zfull)
    ops2 = spread(v2, ysend2, halos2, 14)
    here = 2 * side + core
    for j in range(4):
        for v in range(8):
            bs[pl.ds(j * OWN + 16 * v, 16), :] = v2[pl.ds(v * VEC + 16 * j, 16), :]
        bs[pl.ds(j * OWN + 128, 8), :] = v2[pl.ds(64 + j, 8, stride=VEC), :]
        copy(piece(bs, j), piece(br, here), 19 + j, 19 + here, owner(j)).start()
    row = lax.broadcasted_iota(jnp.int32, (256, 256), 0)
    col = lax.broadcasted_iota(jnp.int32, (256, 256), 1)
    half = jnp.bitwise_and(lax.shift_right_logical(row, 6), 1)
    b_row = 2 * half + lax.shift_right_logical(row, 7)
    z_row = jnp.bitwise_and(row, 63)
    off = z_row - 2 * jnp.bitwise_and(col, 31)
    near = jnp.where(off == 0, 0.5, jnp.where(jnp.logical_or(off == 1, off == -1), 0.25, 0.0))
    main_w = jnp.where(jnp.logical_and(col < 128, lax.shift_right_logical(col, 5) == b_row), near, 0.0)
    next_w = jnp.where(jnp.logical_and(col == 128 + b_row, z_row == 63), 0.25, 0.0)
    wz[...] = (main_w + next_w).astype(BF16)

    gather(sr, srcv)
    collect(ops2)
    laplace(v2, halos2, ops2)

    def residual(rows, m, total):
        after[rows, :] = srcv[rows, :] - total

    operate(residual)

    for i in range(2):
        if i == 0:
            c = [0.5 * vec(after, y) + 0.25 * vec(after, 4 + y) for y in range(4)]
        else:
            c = [0.25 * vec(after, 4 + y) for y in range(4)]
        s3 = 0.25 * swing(c[3])
        d0 = 0.5 * c[0] + 0.25 * c[1] + jnp.where(low, 0.0, s3)
        d1 = 0.5 * c[2] + 0.25 * (c[3] + c[1])
        dn = jnp.where(low, s3, 0.0)
        for r, (da, db) in ((i, (d0, d1)), (2 + i, (dn, None))):
            for h, d in ((0, da), (1, db)):
                if d is None:
                    d = zero_vec
                dh = d.astype(BF16)
                dbuf[pl.ds(r * VEC, VEC), h * 128:(h + 1) * 128] = dh.astype(F32)
                dbuf[pl.ds((4 + r) * VEC, VEC), h * 128:(h + 1) * 128] = d - dh.astype(F32)
    parts = jnp.dot(dbuf[...].astype(BF16), wz[...], preferred_element_type=F32)
    parts = parts[0:4 * VEC] + parts[4 * VEC:8 * VEC]

    def both(r):
        return parts[r * VEC:(r + 1) * VEC, 0:128], parts[r * VEC:(r + 1) * VEC, 128:256]

    lane8 = lanes(8)

    def wide(out, r):
        a, b = both(r)
        for j in range(4):
            out[pl.ds(j * 32, 16), :] = a[16 * j:16 * j + 16]
            out[pl.ds(j * 32 + 16, 8), :] = jnp.where(
                lane8 < 8, b[16 * j:16 * j + 8], pltpu.roll(b[16 * j + 8:16 * j + 16], 8, 1)
            )
            out[pl.ds(j * 32 + 24, 1), :] = a[64 + j:65 + j]
            out[pl.ds(j * 32 + 25, 1), :] = b[64 + j:65 + j]

    def slim(out, r):
        a, b = both(r)
        w = a + pltpu.roll(b, 32, 1)
        for j in range(4):
            out[pl.ds(j * 16, 8), :] = w[16 * j:16 * j + 8] + pltpu.roll(w[16 * j + 8:16 * j + 16], 64, 1)
            out[pl.ds(j * 16 + 8, 1), :] = w[64 + j:65 + j]

    def cut(ref, i, n):
        return ref.at[pl.ds(pl.multiple_of(i * n, 8), n), :]

    def parted(src, dst, n, base, slot, dx, dy):
        return [
            copy(cut(src, j, n), cut(dst, slot, n), base + j, base + slot, (gx + dx, far_gy + dy, j)) for j in range(4)
        ]

    there = 2 * side + 1 - core
    has_xyn = jnp.logical_and(has_xn, has_yn)
    results = []
    for fill, r, src, dst, n, base, slot, dx, dy, cond in (
        (wide, 1, cxs, cxr, 32, 30, there, core, 0, has_xn), (slim, 3, cxys, cxyr, 16, 38, there, core, 1, has_xyn),
        (slim, 2, cys, cyr, 16, 34, here, 0, 1, has_yn), (wide, 0, cms, cmr, 32, 26, here, 0, 0, gx >= 0),
    ):
        fill(src, r)
        ops = parted(src, dst, n, base, slot, dx, dy)
        results.append((cond, ops))

        @pl.when(cond)
        def _():
            for op in ops:
                op.start()

    for j in range(4):
        arrived(piece(br, j), 19 + j, 19 + j)
    for x in range(4):
        c, xl = x // 2, x % 2
        for y in range(4):
            v = 4 * xl + y
            va = br[pl.ds(c * OWN + 16 * v, 16), :]
            vb = br[pl.ds((2 + c) * OWN + 16 * v, 16), :]
            smoothed[pl.ds(x * 8 + y, 16, stride=32), :] = jnp.where(low16, va, swing(vb))
            smoothed[pl.ds(x * 8 + y + 4, 16, stride=32), :] = jnp.where(low16, swing(va), vb)
        ta = br[pl.ds(c * OWN + 128, 8), :]
        tb = br[pl.ds((2 + c) * OWN + 128, 8), :]
        smoothed[pl.ds(512 + x * 8, 4), :] = jnp.where(low8, ta, swing(tb))[4 * xl:4 * xl + 4]
        smoothed[pl.ds(512 + x * 8 + 4, 4), :] = jnp.where(low8, swing(ta), tb)[4 * xl:4 * xl + 4]

    for i in range(4):
        arrived(cut(cmr, i, 32), 26, 26 + i)

        @pl.when(more_x if i % 2 == 0 else gx >= 0)
        def _():
            arrived(cut(cxr, i, 32), 30, 30 + i)

        @pl.when(more_y)
        def _():
            arrived(cut(cyr, i, 16), 34, 34 + i)

        @pl.when(jnp.logical_and(more_x, more_y) if i % 2 == 0 else more_y)
        def _():
            arrived(cut(cxyr, i, 16), 38, 38 + i)

    lane16 = lanes(16)

    def unite(i):
        m = cmr[pl.ds(i * 32, 16), :] + cxr[pl.ds(i * 32, 16), :]
        zp = cmr[pl.ds(i * 32 + 16, 8), :] + cxr[pl.ds(i * 32 + 16, 8), :]
        t = cmr[pl.ds(i * 32 + 24, 8), :] + cxr[pl.ds(i * 32 + 24, 8), :]
        yp = cyr[pl.ds(i * 16, 8), :] + cxyr[pl.ds(i * 16, 8), :]
        yt = cyr[pl.ds(i * 16 + 8, 8), :] + cxyr[pl.ds(i * 16 + 8, 8), :]
        z = jnp.concatenate([zp, pltpu.roll(zp, 120, 1)], 0)
        y = jnp.concatenate([yp, swing(yp)], 0)
        m = m + jnp.where(lane16 < 32, y, 0.0)
        return m, z, y, t + jnp.where(lane8 < 32, yt, 0.0), pltpu.roll(t, 7, 0), yt

    for x in range(2):
        ma, za, ya, ta, zt, yt = unite(x)
        mb, _, _, tb, _, _ = unite(2 + x)
        for b in range(4):
            def joined(left_, right_, extra, edge_y, lane):
                out = jnp.where(lane < 32, pltpu.roll(left_, (128 - 32 * b) % 128, 1), pltpu.roll(right_, (160 - 32 * b) % 128, 1))
                extra = pltpu.roll(extra, 32 - b, 1)
                return out + jnp.where(lane == 32, extra + edge_y if b == 0 else extra, 0.0)

            coarse[pl.ds(x * 4 + b, 16, stride=8), :] = joined(ma, mb, za, ya, lane16)
            coarse[pl.ds(128 + x * 4 + b, 1), :] = joined(ta, tb, zt, yt, lane8)[0:1]

    for j in range(4):
        copy(piece(fs, j), piece(fr, j), j, j, across).wait_send()
        copy(piece(ss, j), piece(sr, j), 4 + j, 4 + j, across).wait_send()
        copy(piece(bs, j), piece(br, j), 19 + j, 19 + j, across).wait_send()
    coefs.wait_send()
    for xn, xp, yn, yp, zc in (ops1, ops2):
        zc.wait_send()
        for cond, op in ((has_xn, xn), (has_xp, xp), (has_yn, yn), (has_yp, yp)):
            @pl.when(cond)
            def _():
                op.wait_send()
    for cond, ops in results:
        @pl.when(cond)
        def _():
            for op in ops:
                op.wait_send()


def scratch():
    def rows(n, width=128, kind=F32):
        return pltpu.VMEM((n, width), kind)

    halos = [rows(4 * VEC), rows(4 * VEC), rows(VEC), rows(VEC), rows(16)]
    return [
        rows(SL * 32), rows(SL * 32), rows(32), rows(TERMS * 32), pltpu.VMEM((TERMS, 3, 4 * SL), jnp.int32),
        pltpu.VMEM((TERMS, 3, 4 * SL), F32), pltpu.SemaphoreType.DMA((7,)),
        rows(4 * OWN), rows(4 * OWN), rows(8 * (TERMS + 1)), rows(4 * OWN), rows(4 * OWN), rows(8 * (TERMS + 1)),
        rows(ALL), rows(ALL), *halos, *halos, rows(VEC), rows(2 * VEC + 16), rows(2 * VEC + 16), rows(ALL), rows(4 * 256, 256, BF16),
        rows(TERMS * VEC, 256), rows(TERMS * VEC, 256, BF16), rows(128), rows(128), rows(ALL), rows(ALL), rows(256, 256, BF16),
        rows(4 * OWN), rows(4 * OWN), rows(8 * VEC, 256), rows(8), rows(128), rows(128), rows(64), rows(64),
        rows(128), rows(128), rows(64), rows(64),
        pltpu.SemaphoreType.DMA((42,)), pltpu.SemaphoreType.DMA((42,)),
    ]


def store(smoothed, coarse, smoothed_out, coarse_out, sems):
    ops = [
        pltpu.make_async_copy(smoothed, smoothed_out, sems.at[0]), pltpu.make_async_copy(coarse, coarse_out, sems.at[1]),
    ]
    for op in ops:
        op.start()
    for op in ops:
        op.wait()


def body(field, source, mean_coef, var_coefs, galerkin_cols, galerkin_vals):
    whole = pl.BlockSpec(memory_space=pltpu.VMEM)
    smoothed, coarse = pl.pallas_call(
        kernel,
        out_shape=(pltpu.VMEM((SL * 32, 128), F32), pltpu.VMEM((SL * 8, 128), F32)),
        in_specs=[pl.BlockSpec(memory_space=pl.ANY)] * 6,
        out_specs=(whole, whole),
        scratch_shapes=scratch(),
        compiler_params=pltpu.CompilerParams(collective_id=0, has_side_effects=True),
        name="sweep",
    )(
        field.reshape(SL * 32, 128), source.reshape(SL * 32, 128), mean_coef.reshape(32, 128),
        var_coefs.reshape(TERMS * 32, 128), jnp.swapaxes(galerkin_cols, 1, 2), jnp.swapaxes(galerkin_vals, 1, 2),
    )
    anywhere = pl.BlockSpec(memory_space=pl.ANY)
    smoothed, coarse = pl.pallas_call(
        store,
        out_shape=(jax.ShapeDtypeStruct((SL * 32, 128), F32), jax.ShapeDtypeStruct((SL * 8, 128), F32)),
        in_specs=[whole] * 2,
        out_specs=(anywhere, anywhere),
        scratch_shapes=[pltpu.SemaphoreType.DMA((2,))],
        name="store",
    )(pltpu.with_memory_space_constraint(smoothed, pltpu.VMEM), pltpu.with_memory_space_constraint(coarse, pltpu.VMEM))
    return smoothed.reshape(field.shape), coarse[:, 0:64].reshape(SL, 2, 4, 64)


def solution(mesh):
    wide = P("chaos", "gx", "gy", None)
    return jax.shard_map(
        body,
        mesh=mesh,
        in_specs=(wide, wide, P("gx", "gy", None), P(None, "gx", "gy", None), P(), P()),
        out_specs=(wide, wide),
        check_vma=False,
    )
```
